512 devices in a mesh: tensor: 8 (over y, core), context: 64 (over x, z).
Axes of the slice: x: 4, y: 4, z: 16, core: 2. Of those that a mesh axis runs over, the one named last changes fastest.
Arguments:
- queries: bfloat16 [16384, 6144], P('context', 'tensor'), as said below
- key_states: bfloat16 [16384, 1024], P('context', 'tensor'), as said below
- value_states: bfloat16 [16384, 1024], P('context', 'tensor'), may hold values from -6 to 6
- sentence_lengths: int32 [1024], replicated, may hold values from 1 to 64, 16384 in all
- sentence_owner: int32 [1024, 1], replicated, may hold values from 0 to 63; in each aligned block of 1024 rows (0 to 1023, 1024 to 2047, ...) at most 24 rows name the same one
- answer_start: int32 [1], replicated, may hold values from 8192 to 16256
Outputs:
- attention: bfloat16 [16384, 6144], P('context', 'tensor')
- citations: float32 [1536, 128], P('context', 'tensor')
The draws below stay inside these ranges and needn't reach their ends.
Inputs may be any that keep to these rules, and one draw needn't show every extreme that they name: queries lie within -36 to 36. key_states lie within -12 to 12. `sentence_lengths`: each sentence has 1 to 64 tokens, one exactly 64, and they sum to 16384. `sentence_owner`: no index of context owns more than 24 sentences, and one owns exactly 24. `answer_start`: the answer rows fit in the document.
All inputs are finite; a program needn't handle non-finite values.
Results may differ from the reference program's by a relative error of at most 0.022.
Values may be sent and summed in bfloat16 or wider, within the bound.
No kernel may reach another device: no remote copies, remote signals or barrier semaphores. Data moves between devices by JAX's collectives and lax.ppermute only.
A program may use at most 64 MiB of HBM per device.

```python
import math
import jax
import jax.numpy as jnp
import numpy as np
from jax import lax

HEAD = 128
QH_GROUP = 6
TOK_DEV = 256
ANS = 128
SENT_DEV = 16
SENT_MAX = 64
SPAN = 128
TOKENS = 16384
KV_HEADS = 8
HEADS = 48
S_TOT = 1024
SENT_OWN = 24
OWNER_ROWS = 1536
N_CONTEXT = 64


def draw_key_states(key, part):
    drawn = jax.random.normal(jax.random.fold_in(key, 12), (TOKENS, KV_HEADS * HEAD), jnp.float32)
    drawn = jnp.clip(drawn, -6.0, 6.0)
    return drawn.astype(jnp.bfloat16)


def draw_queries(key, part):
    drawn = jax.random.normal(jax.random.fold_in(key, 11), (TOKENS, HEADS * HEAD), jnp.float32)
    drawn = jnp.clip(drawn, -6.0, 6.0)
    return drawn.astype(jnp.bfloat16)


def levels(rng, dims, cuts, low, high):
    level, own = 1.0, jax.random.fold_in(rng, 6)
    for dim, blocks in cuts:
        draws = jnp.exp(jax.random.uniform(jax.random.fold_in(own, dim), (blocks,), jnp.float32, low / len(cuts), high / len(cuts)))
        level = level * jnp.repeat(draws, dims[dim] // blocks).reshape([-1 if axis == dim else 1 for axis in range(len(dims))])
    return level


def split_up(number_of, total, reach, lean):
    loads = [(1 << 20) // math.isqrt(standing ** lean) + 1 for standing in range(2, number_of + 1)]
    surplus, counts = total - reach - (number_of - 1), [1] * (number_of - 1)
    while surplus > 0:
        candidates = [i for i in range(number_of - 1) if counts[i] < reach]
        pool, left = sum([loads[i] for i in candidates]), surplus
        for i in candidates:
            extra = min(reach - counts[i], max(1, left * loads[i] // pool), surplus)
            counts[i] = counts[i] + extra
            surplus = surplus - extra
    return np.array([reach] + counts)


def ragged(rng, amount, total, most, slope):
    if amount == 2:
        one = jax.random.randint(rng, (), max(1, total - most), min(most, total - 1) + 1)
        return jnp.stack([one, total - one])
    tallies = jnp.asarray(split_up(amount, total, most, slope), jnp.int32)
    pairs = (amount - 1) // 2
    giver, receiver = tallies[1:1 + 2 * pairs:2], tallies[2:2 + 2 * pairs:2]
    margin = jnp.minimum(giver - 1, most - receiver)
    shifted = jax.random.randint(jax.random.fold_in(rng, 1), (pairs,), 0, 1 << 20) % (margin + 1)
    tallies = tallies.at[1:1 + 2 * pairs:2].set(giver - shifted).at[2:2 + 2 * pairs:2].set(receiver + shifted)
    return tallies[jax.random.permutation(jax.random.fold_in(rng, 2), amount)]


def assign_block(rng, own, number, rows, number_of, top, limit, lean):
    order = jax.random.permutation(rng, number_of)
    packed, usual = portions_of(number_of, rows * top, limit, lean, True), portions_of(number_of, rows * top, limit, lean, False)
    places = jnp.arange(number_of)

    def named(sizes, offset_by):
        used = int((sizes > 0).sum())
        fixed = max(1, used // 4)
        shifted = fixed + (places - fixed + offset_by * (used - fixed)) % max(1, number_of - fixed)
        return jnp.zeros((number_of,), jnp.int32).at[order[jnp.where(places < fixed, places, shifted)]].set(jnp.asarray(sizes, jnp.int32))

    sizes = jnp.where(number % 4 == 0, named(packed, number // 4), named(usual, number - number // 4 - 1))
    mixed = jax.random.permutation(jax.random.fold_in(own, 3), number_of)
    donor, sink = mixed[0:number_of // 2 * 2:2], mixed[1:number_of // 2 * 2:2]
    slack = jnp.minimum(sizes[donor] - 1, limit - sizes[sink]) // 2
    slack = jnp.where((donor == order[0]) | (sink == order[0]) | (sizes[sink] == 0), 0, jnp.maximum(slack, 0))
    shifted = jax.random.randint(jax.random.fold_in(own, 4), (number_of // 2,), 0, 1 << 20) % (slack + 1)
    sizes = sizes.at[donor].add(-shifted).at[sink].add(shifted)
    members = jnp.searchsorted(jnp.cumsum(sizes), jnp.arange(rows * top), side="right").astype(jnp.int32)
    table = members.reshape(top, rows).T
    table = table[jax.random.permutation(jax.random.fold_in(own, 1), rows)]
    offset_by = jax.random.randint(jax.random.fold_in(own, 2), (rows, 1), 0, top)
    return jnp.take_along_axis(table, (jnp.arange(top)[None, :] + offset_by) % top, axis=1)


def portions_of(number_of, total, most, slope, full):
    loads = [(1 << 20) // math.isqrt(standing ** slope) + 1 for standing in range(1, number_of + 1)]
    largest = most if full else min(most, max(-(-total // number_of), total * loads[0] // sum(loads)))
    least = 1 if total - largest >= number_of - 1 else 0
    given, rest = [largest] + [least] * (number_of - 1), total - largest - least * (number_of - 1)
    while rest > 0:
        movable = [i for i in range(1, number_of) if given[i] < largest] or [i for i in range(1, number_of) if given[i] < most]
        whole, budget = sum([loads[i] for i in movable]), rest
        for i in movable:
            more = min(most - given[i], max(1, budget * loads[i] // whole), rest)
            given[i] = given[i] + more
            rest = rest - more
    return np.array(given)


def normal_values(stream_key, extent, scale, most, pieces=(), held_as=jnp.bfloat16):
    values = scale * jax.random.normal(stream_key, extent, jnp.float32)
    if pieces:
        values = values * levels(stream_key, extent, pieces, -0.22, 0.18)
    return jnp.clip(values, -most, most).astype(held_as)


def setup_inputs(seed: int = 0) -> dict:
    keys = jax.random.split(jax.random.key(seed), 7)
    queries = draw_queries(jax.random.fold_in(keys[6], 71), 0)
    key_states = draw_key_states(jax.random.fold_in(keys[6], 71), 0)
    value_states = normal_values(keys[2], (TOKENS, KV_HEADS * HEAD), 1.0, 6.0, ((0, 64), (1, 8)))
    sentence_lengths = ragged(keys[3], S_TOT, TOKENS, SENT_MAX, 2).astype(jnp.int32)
    sentence_owner_keys = jax.random.split(jax.random.fold_in(keys[4], 1), S_TOT // S_TOT)
    sentence_owner_turns = jax.random.permutation(jax.random.fold_in(keys[4], 3), S_TOT // S_TOT)
    sentence_owner = jax.vmap(lambda own, number: assign_block(jax.random.fold_in(keys[4], 2), own, number, S_TOT, N_CONTEXT, 1, SENT_OWN, 2))(sentence_owner_keys, sentence_owner_turns).reshape((S_TOT, 1))
    answer_start = jax.random.randint(keys[5], (1,), TOKENS // 2, TOKENS - ANS + 1).astype(jnp.int32)
    return dict(queries=queries, key_states=key_states, value_states=value_states, sentence_lengths=sentence_lengths, sentence_owner=sentence_owner, answer_start=answer_start)


def storage_positions(count):
    rows = jnp.arange(count, dtype=jnp.int32)
    owner_dev = rows // TOK_DEV
    upper = (rows % TOK_DEV) // SPAN
    within = rows % SPAN
    piece_id = jnp.where(upper == 0, owner_dev, 2 * N_CONTEXT - 1 - owner_dev)
    return piece_id * SPAN + within


def rows_of_positions(count):
    places = jnp.arange(count, dtype=jnp.int32)
    piece_id = places // SPAN
    within = places % SPAN
    owner_dev = jnp.where(piece_id < N_CONTEXT, piece_id, 2 * N_CONTEXT - 1 - piece_id)
    upper = (piece_id >= N_CONTEXT).astype(jnp.int32)
    return owner_dev * TOK_DEV + upper * SPAN + within


def reference(queries, key_states, value_states, sentence_lengths, sentence_owner, answer_start):
    total = TOKENS
    order = rows_of_positions(total)
    query_pos = jnp.take(queries, order, axis=0)
    key_pos = jnp.take(key_states, order, axis=0)
    value_pos = jnp.take(value_states, order, axis=0)
    score_scale = 1.0 / (HEAD ** 0.5)
    block_rows = min(total, max(1024, total // 16))

    def group_attention(group_index):
        query_group = lax.dynamic_slice_in_dim(query_pos, group_index * QH_GROUP * HEAD, QH_GROUP * HEAD, 1)
        query_group = query_group.reshape(total, QH_GROUP, HEAD)
        key_group = lax.dynamic_slice_in_dim(key_pos, group_index * HEAD, HEAD, 1)
        value_group = lax.dynamic_slice_in_dim(value_pos, group_index * HEAD, HEAD, 1)
        outputs = []
        log_totals = []
        for block_index in range(total // block_rows):
            low_row = block_index * block_rows
            high_row = low_row + block_rows
            query_block = query_group[low_row:high_row].transpose(1, 0, 2).reshape(QH_GROUP * block_rows, HEAD)
            key_block = key_group[:high_row]
            value_block = value_group[:high_row]
            scores = lax.dot_general(query_block, key_block, (((1,), (1,)), ((), ())), preferred_element_type=jnp.float32) * score_scale
            query_place = jnp.tile(jnp.arange(low_row, high_row, dtype=jnp.int32), QH_GROUP)
            key_place = jnp.arange(high_row, dtype=jnp.int32)
            visible = key_place[None, :] <= query_place[:, None]
            row_best = jnp.max(jnp.where(visible, scores, -1e30), axis=1)
            expon = jnp.where(visible, jnp.exp(scores - row_best[:, None]), 0.0)
            row_total = jnp.sum(expon, axis=1)
            mixed = jnp.dot(expon.astype(jnp.bfloat16), value_block, preferred_element_type=jnp.float32)
            normed = (mixed / row_total[:, None]).astype(jnp.bfloat16)
            outputs.append(normed.reshape(QH_GROUP, block_rows, HEAD).transpose(1, 0, 2).reshape(block_rows, QH_GROUP * HEAD))
            log_totals.append((row_best + jnp.log(row_total)).reshape(QH_GROUP, block_rows).T)
        return jnp.concatenate(outputs, axis=0), jnp.concatenate(log_totals, axis=0)

    attn_groups, lse_groups = lax.map(group_attention, jnp.arange(KV_HEADS, dtype=jnp.int32))
    attn_pos = attn_groups.transpose(1, 0, 2).reshape(total, HEADS * HEAD)
    lse_pos = lse_groups.transpose(1, 0, 2).reshape(total, HEADS)
    attention = jnp.take(attn_pos, storage_positions(total), axis=0)

    start_row = answer_start[0].astype(jnp.int32)
    answer_pos = start_row + jnp.arange(ANS, dtype=jnp.int32)
    answer_queries = lax.dynamic_slice_in_dim(query_pos, start_row, ANS, 0)
    answer_lse = lax.dynamic_slice_in_dim(lse_pos, start_row, ANS, 0)
    starts = jnp.cumsum(sentence_lengths) - sentence_lengths
    places = jnp.arange(total, dtype=jnp.int32)
    sentence_of = jnp.sum((starts[None, :] <= places[:, None]).astype(jnp.int32), axis=1) - 1
    owners = sentence_owner[:, 0]
    counter = jnp.arange(S_TOT, dtype=jnp.int32)
    same_owner = (owners[None, :] == owners[:, None]) & (counter[None, :] < counter[:, None])
    slots = jnp.sum(same_owner.astype(jnp.int32), axis=1)
    targets = owners * SENT_OWN + slots
    token_target = jnp.take(targets, sentence_of)
    onehot_rows = (token_target[:, None] == jnp.arange(OWNER_ROWS, dtype=jnp.int32)[None, :]).astype(jnp.bfloat16)
    visible = places[None, :] <= answer_pos[:, None]
    visible_all = jnp.tile(visible, (QH_GROUP, 1))

    def group_cite(group_index):
        query_group = lax.dynamic_slice_in_dim(answer_queries, group_index * QH_GROUP * HEAD, QH_GROUP * HEAD, 1)
        query_group = query_group.reshape(ANS, QH_GROUP, HEAD).transpose(1, 0, 2).reshape(QH_GROUP * ANS, HEAD)
        lse_group = lax.dynamic_slice_in_dim(answer_lse, group_index * QH_GROUP, QH_GROUP, 1).T.reshape(QH_GROUP * ANS)
        key_group = lax.dynamic_slice_in_dim(key_pos, group_index * HEAD, HEAD, 1)
        scores = lax.dot_general(query_group, key_group, (((1,), (1,)), ((), ())), preferred_element_type=jnp.float32) * score_scale
        prob = jnp.where(visible_all, jnp.exp(scores - lse_group[:, None]), 0.0).astype(jnp.bfloat16)
        pooled = jnp.dot(prob, onehot_rows, preferred_element_type=jnp.float32)
        return jnp.sum(pooled.reshape(QH_GROUP, ANS, OWNER_ROWS), axis=0)

    pooled_all = jnp.sum(lax.map(group_cite, jnp.arange(KV_HEADS, dtype=jnp.int32)), axis=0)
    factor = (answer_pos + 1).astype(jnp.float32) * (SENT_DEV / (TOK_DEV * HEADS))
    citations = (pooled_all * factor[:, None]).T
    return attention, citations
```

```python
import functools
import math

import jax
import jax.numpy as jnp
from jax import lax
from jax.experimental import pallas as pl
from jax.experimental.pallas import tpu as pltpu
from jax.sharding import Mesh, PartitionSpec as P

HEAD = 128
GROUP = 6
SPAN = 128
ANS = 128
SENT_DEV = 16
SENT_OWN = 24
NX = 4
NZ = 16
N_CONTEXT = NX * NZ
N_TENSOR = 8
PIECES = 2 * N_CONTEXT
TOK_DEV = 2 * SPAN
HEADS = GROUP * N_TENSOR
S_TOT = 1024
KEYS_HALF = NZ * SPAN
SET_ROWS = GROUP * SPAN
NKM = 512
RB = 256
SLOT_PAD = 32
ANS_X = ANS // NX
TAIL = 16 + SLOT_PAD
LOW = -1e30
TINY = 1e-37
SCALE2 = math.log2(math.e) / math.sqrt(HEAD)
F32 = jnp.float32
BF16 = jnp.bfloat16

DOT_LAST = (((1,), (1,)), ((), ()))


def lanes(value):
    return jnp.broadcast_to(value, (value.shape[0], 128))


def prep_kernel(ids, len_ref, own_ref, out_ref):
    lengths = len_ref[...].astype(F32)
    owner = own_ref[...]
    before = (
        lax.broadcasted_iota(jnp.int32, (S_TOT, S_TOT), 0)
        < lax.broadcasted_iota(jnp.int32, (S_TOT, S_TOT), 1)
    ).astype(F32).astype(BF16)
    lengths = jnp.broadcast_to(lengths, (8, S_TOT))
    starts = jnp.dot(lengths.astype(BF16), before, preferred_element_type=F32)
    owned = (lax.broadcasted_iota(jnp.int32, (N_CONTEXT, S_TOT), 0) == owner).astype(F32)
    earlier = jnp.dot(owned.astype(BF16), before, preferred_element_type=F32)
    slots = jnp.sum(owned * earlier, axis=0, keepdims=True).astype(jnp.int32)
    place = jnp.where(owner % NZ == ids[1], owner // NZ * SLOT_PAD + slots, -1)
    hit = (lax.broadcasted_iota(jnp.int32, (128, S_TOT), 0) == place).astype(F32).astype(BF16)
    high = jnp.floor(starts * (1.0 / 128.0))
    low = starts - high * 128.0
    row = lax.broadcasted_iota(jnp.int32, (8, S_TOT), 0)
    parts = jnp.where(row == 0, high, jnp.where(row == 1, low, lengths))
    placed = lax.dot_general(parts.astype(BF16), hit, DOT_LAST, preferred_element_type=F32)
    start = placed[0:1] * 128.0 + placed[1:2]
    end = start + placed[2:3]
    row_out = lax.broadcasted_iota(jnp.int32, (8, 128), 0)
    out_ref[...] = jnp.where(row_out == 0, start, end).astype(jnp.int32)


def pick_kernel(ids, *refs):
    q_refs, out_ref = refs[:NX], refs[NX]
    my_x, my_z, start = ids[0], ids[1], ids[2]
    row = lax.broadcasted_iota(jnp.int32, (ANS_X, SPAN), 0)
    lane = lax.broadcasted_iota(jnp.int32, (ANS_X, SPAN), 1)
    value = None
    for j in range(NX):
        other_x = lax.rem(my_x - j + NX, NX)
        piece = PIECES - 1 - (other_x * NZ + my_z)
        pick = (piece * SPAN + lane == start + my_x * ANS_X + row).astype(F32).astype(BF16)
        part = jnp.dot(pick, q_refs[j][SPAN:TOK_DEV, :], preferred_element_type=F32)
        value = part if value is None else value + part
    out_ref[...] = value.astype(BF16)


def unit(queries, keys, values, state, index, visible):
    best, total, accum = state
    width = keys.shape[0]
    for rb in range(SET_ROWS // RB):
        rows = slice(rb * RB, (rb + 1) * RB)
        raw = lax.dot_general(queries(rows), keys, DOT_LAST, preferred_element_type=F32)
        parts = [raw[:, i * 128 : (i + 1) * 128] * SCALE2 for i in range(width // 128)]
        if visible is not None:
            parts = [jnp.where(v, p, LOW) for v, p in zip(visible, parts)]
        top = functools.reduce(jnp.maximum, parts)
        old = best[index, rows, :]
        new = jnp.maximum(old, lanes(jnp.max(top, axis=1, keepdims=True)))
        alpha = jnp.exp2(old - new)
        weights = jnp.concatenate([jnp.exp2(p - new).astype(BF16) for p in parts], axis=1)
        mixed = jnp.dot(weights, values, preferred_element_type=F32)
        best[index, rows, :] = new
        total[index, rows, :] = total[index, rows, :] * alpha + mixed[:, HEAD:]
        accum[index, rows, :] = accum[index, rows, :] * alpha + mixed[:, :HEAD]


def reset(state):
    best, total, accum = state
    best[...] = jnp.full_like(best, LOW)
    total[...] = jnp.zeros_like(total)
    accum[...] = jnp.zeros_like(accum)


def limits_to_masks(limits):
    row_w = lax.broadcasted_iota(jnp.int32, (RB, 128), 0) % SPAN
    offset = lax.broadcasted_iota(jnp.int32, (RB, 128), 1) - row_w
    return [offset <= limit for limit in limits]


def pack_logs(logs):
    flipped = logs.T[0:8, :]
    hi = flipped.astype(BF16)
    rest = flipped - hi.astype(F32)
    mid = rest.astype(BF16)
    lo = (rest - mid.astype(F32)).astype(BF16)
    return jnp.concatenate([hi, mid, lo], axis=1)


def read_logs(packed):
    packed = packed.astype(F32)
    return packed[:, :128] + packed[:, 128:256] + packed[:, 256:384]


def finish(state, index, write):
    best, total, accum = state
    lane = lax.broadcasted_iota(jnp.int32, (SPAN, 128), 1)
    logs = jnp.zeros((SPAN, 128), F32)
    for h in range(GROUP):
        rows = slice(h * SPAN, (h + 1) * SPAN)
        tot = jnp.maximum(total[index, rows, :], TINY)
        logs = jnp.where(lane == h, best[index, rows, :] + jnp.log2(tot), logs)
        write(h, accum[index, rows, :] / tot)
    return pack_logs(logs)


def others_kernel(*refs):
    ids, table = refs[0:2]
    q_refs = refs[2 : 1 + NX]
    a_refs = refs[1 + NX : 1 + 2 * NX]
    kv_ref = refs[1 + 2 * NX]
    msg_refs = refs[2 + 2 * NX : 1 + 3 * NX]
    own_ref = refs[1 + 3 * NX]
    qs, ks, vs, flat = refs[2 + 3 * NX : 6 + 3 * NX]
    state = refs[6 + 3 * NX :]
    my_x, my_z, start = ids[0], ids[1], ids[2]
    cited = 2 * NX - 2
    other_x = [lax.rem(my_x - j + NX, NX) for j in range(NX)]

    for j in range(1, NX):
        for half in range(2):
            for h in range(GROUP):
                qs[2 * j - 2 + half, h * SPAN : (h + 1) * SPAN, :] = q_refs[j - 1][
                    half * SPAN : (half + 1) * SPAN, h * HEAD : (h + 1) * HEAD
                ]
    for j in range(NX):
        for h in range(GROUP):
            at = pl.ds(pl.multiple_of(h * ANS + other_x[j] * ANS_X, ANS_X), ANS_X)
            qs[cited, at, :] = a_refs[j][:, h * HEAD : (h + 1) * HEAD]
    col = lax.broadcasted_iota(jnp.int32, (SPAN, 128), 0)
    ones = jnp.ones((SPAN, HEAD), BF16)

    def bases(slot):
        context = my_x * NZ + slot
        return context * SPAN, (PIECES - 1 - context) * SPAN

    for slot in range(NZ):
        for half in range(2):
            block = kv_ref[slot * TOK_DEV + half * SPAN : slot * TOK_DEV + (half + 1) * SPAN, :]
            rows = slice(slot * SPAN, (slot + 1) * SPAN)
            ks[half, rows, :] = block[:, :HEAD]
            vs[0, half, rows, 0:HEAD] = block[:, HEAD:]
            vs[0, half, rows, HEAD:] = ones
            place = bases(slot)[half] + col
            inside = jnp.logical_and(place >= table[0:1, :], place < table[1:2, :])
            vs[1, half, rows, 0:HEAD] = inside.astype(F32).astype(BF16)
            vs[1, half, rows, HEAD:] = ones
    reset(state)

    def step(index, kind, half, visible):
        unit(
            lambda rows: qs[index, rows, :], ks[half], vs[kind, half], state, index, visible
        )

    def first(i, carry):
        step(4 * i + 1, 0, 0, None)
        step(jnp.where(i == 0, 3, cited), i, 0, None)
        return carry

    lax.fori_loop(0, 2, first, 0)
    high = [(x < my_x).astype(jnp.int32) for x in other_x]
    step(high[1], 0, high[1], None)
    step(2 + high[2], 0, high[2], None)
    step(4 + high[3], 0, high[3], None)

    @pl.when(bases(NZ - 1)[1] < start + ANS)
    def _():
        limits = [start - bases(slot)[1] for slot in range(NZ)]
        step(cited, 1, 1, limits_to_masks(limits))

    def keep(h, value):
        flat[:, h * ANS : (h + 1) * ANS] = value.T.astype(BF16)

    cited_logs = finish(state, cited, keep)
    for j in range(NX):
        if j == 0:
            tail = own_ref
        else:
            tail = msg_refs[j - 1].at[TOK_DEV : TOK_DEV + TAIL]
            for half in range(2):

                def write(h, value):
                    msg_refs[j - 1][
                        half * SPAN : (half + 1) * SPAN, h * HEAD : (h + 1) * HEAD
                    ] = value.astype(BF16)

                tail[0:8, half * 384 : half * 384 + 384] = finish(state, 2 * j - 2 + half, write)
        tail[8:16, 0:384] = cited_logs
        tail[16:TAIL, :] = flat[pl.ds(pl.multiple_of(other_x[j] * SLOT_PAD, SLOT_PAD), SLOT_PAD), :]


def own_kernel(ids, q_ref, kv_ref, msg_ref, qs, ks, vs, *state):
    my_z = ids[1]
    per = NKM // SPAN
    ones = jnp.ones((SPAN, HEAD), BF16)
    for half in range(2):
        for h in range(GROUP):
            qs[half, h * SPAN : (h + 1) * SPAN, :] = q_ref[
                half * SPAN : (half + 1) * SPAN, h * HEAD : (h + 1) * HEAD
            ]
        for slot in range(NZ):
            block = kv_ref[slot * TOK_DEV + half * SPAN : slot * TOK_DEV + (half + 1) * SPAN, :]
            rows = slice(slot * SPAN, (slot + 1) * SPAN)
            ks[half, rows, :] = block[:, :HEAD]
            vs[half, rows, 0:HEAD] = block[:, HEAD:]
            vs[half, rows, HEAD:] = ones
    reset(state)
    unit(lambda rows: qs[1, rows, :], ks[0], vs[0], state, 1, None)

    def masked(half, g):
        limits = []
        for i in range(per):
            slot = g * per + i
            seen = slot < my_z if half == 0 else slot > my_z
            limits.append(jnp.where(slot == my_z, 0, jnp.where(seen, SPAN, -SPAN)))
        at = pl.ds(pl.multiple_of(g * NKM, NKM), NKM)
        unit(
            lambda rows: qs[half, rows, :],
            ks[half, at, :],
            vs[half, at, :],
            state,
            half,
            limits_to_masks(limits),
        )

    def low(g, carry):
        masked(0, g)
        return carry

    def high(g, carry):
        masked(1, g)
        return carry

    lax.fori_loop(0, my_z // per + 1, low, 0)
    lax.fori_loop(my_z // per, NZ // per, high, 0)
    for half in range(2):

        def write(h, value):
            msg_ref[half * SPAN : (half + 1) * SPAN, h * HEAD : (h + 1) * HEAD] = value.astype(BF16)

        msg_ref[TOK_DEV : TOK_DEV + 8, half * 384 : half * 384 + 384] = finish(state, half, write)


def shares_of(logs):
    top = functools.reduce(jnp.maximum, logs)
    shares = [jnp.exp2(v - top) for v in logs]
    tot = functools.reduce(jnp.add, shares)
    return [v / tot for v in shares]


def combine_kernel(ids, *refs):
    msgs = refs[:NX]
    own_cited, out_ref, cite_ref = refs[NX:]
    tails = [own_cited] + [m.at[TOK_DEV : TOK_DEV + TAIL] for m in msgs[1:]]
    pad = jnp.zeros((SPAN - 8, SPAN), F32)
    for half in range(2):
        logs = slice(half * 384, half * 384 + 384)
        shares = shares_of([read_logs(m[TOK_DEV : TOK_DEV + 8, logs]) for m in msgs])
        flipped = [jnp.concatenate([v, pad], axis=0).T for v in shares]
        rows = slice(half * SPAN, (half + 1) * SPAN)
        for h in range(GROUP):
            cols = slice(h * HEAD, (h + 1) * HEAD)
            pieces = [
                m[rows, cols].astype(F32) * lanes(f[:, h : h + 1]) for m, f in zip(msgs, flipped)
            ]
            out_ref[rows, cols] = functools.reduce(jnp.add, pieces).astype(BF16)
    shares = shares_of([read_logs(t[8:16, 0:384]) for t in tails])
    value = jnp.zeros((SLOT_PAD, ANS), F32)
    for tail, share in zip(tails, shares):
        for h in range(GROUP):
            block = tail[16:TAIL, h * ANS : (h + 1) * ANS].astype(F32)
            value = value + block * share[h : h + 1, :]
    row = lax.broadcasted_iota(jnp.int32, (SLOT_PAD, ANS), 1)
    factor = (ids[2] + row + 1).astype(F32) * (SENT_DEV / (TOK_DEV * HEADS))
    value = value * factor
    for t in range(N_TENSOR):
        cite_ref[t] = value[0:SENT_OWN, :]


VMEM_SPEC = pl.BlockSpec(memory_space=pltpu.VMEM)
SMEM_SPEC = pl.BlockSpec(memory_space=pltpu.SMEM)


def call(kernel, name, out_shape, scalars, arrays, scratch=(), flops=1e6, moved=1e6):
    many = isinstance(out_shape, list)
    return pl.pallas_call(
        kernel,
        out_shape=out_shape,
        in_specs=[SMEM_SPEC] * scalars + [VMEM_SPEC] * arrays,
        out_specs=[VMEM_SPEC] * len(out_shape) if many else VMEM_SPEC,
        scratch_shapes=list(scratch),
        compiler_params=pltpu.CompilerParams(vmem_limit_bytes=40 << 20),
        cost_estimate=pl.CostEstimate(
            flops=int(flops), bytes_accessed=int(moved), transcendentals=0
        ),
        name=name,
    )


def ring(count, step):
    return [(i, (i + step) % count) for i in range(count)]


def per_device(queries, key_states, value_states, sentence_lengths, sentence_owner, answer_start):
    my_x = lax.axis_index("x")
    my_z = lax.axis_index("z")
    ids = jnp.stack([my_x, my_z, answer_start[0]]).astype(jnp.int32)

    table = call(
        prep_kernel, "prep", jax.ShapeDtypeStruct((8, 128), jnp.int32), 1, 2, flops=3e8, moved=2e4
    )(ids, sentence_lengths.reshape(1, S_TOT), sentence_owner.reshape(1, S_TOT))

    pairs = lax.all_gather(
        jnp.concatenate([key_states, value_states], axis=1), "z", axis=0, tiled=True
    )
    q_all = [queries] + [lax.ppermute(queries, "x", ring(NX, j)) for j in (1, 2, 3)]
    asked = call(
        pick_kernel, "pick", jax.ShapeDtypeStruct((ANS_X, GROUP * HEAD), BF16), 1, NX, flops=3e7
    )(ids, *q_all)
    for shifts in ((8,), (4,), (2, 1, -1)):
        got = [lax.ppermute(asked, "z", ring(NZ, s)) for s in shifts]
        asked = functools.reduce(jnp.add, got, asked)
    asked_all = [asked] + [lax.ppermute(asked, "x", ring(NX, j)) for j in (1, 2, 3)]

    wide = jax.ShapeDtypeStruct((TOK_DEV + TAIL, GROUP * HEAD), BF16)
    sets = 2 * NX - 1
    out = call(
        others_kernel,
        "attend_others",
        [wide] * (NX - 1) + [jax.ShapeDtypeStruct((TAIL, GROUP * HEAD), BF16)],
        1,
        2 * NX + 1,
        [
            pltpu.VMEM((sets, SET_ROWS, HEAD), BF16),
            pltpu.VMEM((2, KEYS_HALF, HEAD), BF16),
            pltpu.VMEM((2, 2, KEYS_HALF, 2 * HEAD), BF16),
            pltpu.VMEM((128, GROUP * ANS), BF16),
        ]
        + [pltpu.VMEM((sets, SET_ROWS, 128), F32)] * 3,
        flops=8e9,
        moved=6e6,
    )(ids, table, *q_all[1:], *asked_all, pairs)
    sent, own_cited = out[: NX - 1], out[NX - 1]
    got = [lax.ppermute(sent[j - 1], "x", ring(NX, -j)) for j in (1, 2, 3)]
    own = call(
        own_kernel,
        "attend_own",
        jax.ShapeDtypeStruct((TOK_DEV + 16, GROUP * HEAD), BF16),
        1,
        2,
        [
            pltpu.VMEM((2, SET_ROWS, HEAD), BF16),
            pltpu.VMEM((2, KEYS_HALF, HEAD), BF16),
            pltpu.VMEM((2, KEYS_HALF, 2 * HEAD), BF16),
        ]
        + [pltpu.VMEM((2, SET_ROWS, 128), F32)] * 3,
        flops=2e9,
        moved=3e6,
    )(ids, queries, pairs)

    attention, cited = call(
        combine_kernel,
        "combine",
        [
            jax.ShapeDtypeStruct((TOK_DEV, GROUP * HEAD), BF16),
            jax.ShapeDtypeStruct((N_TENSOR, SENT_OWN, ANS), F32),
        ],
        1,
        NX + 1,
        flops=1e7,
        moved=3e6,
    )(ids, own, *got, own_cited)

    parts = jnp.sum(lax.all_to_all(cited, ("y", "core"), 0, 0), axis=0)
    share = ANS // N_TENSOR
    first = (lax.axis_index("y") * 2 + lax.axis_index("core")) * share
    citations = lax.dynamic_slice_in_dim(parts, first, share, 1)
    return (attention, citations)


def solution(mesh):
    grid = Mesh(mesh.devices.reshape(NX, 2, NX, NZ), ("y", "core", "x", "z"))
    context, tensor = ("x", "z"), ("y", "core")
    return jax.shard_map(
        per_device,
        mesh=grid,
        in_specs=(
            P(context, tensor),
            P(context, tensor),
            P(context, tensor),
            P(),
            P(),
            P(),
        ),
        out_specs=(P(context, tensor), P(context, tensor)),
        check_vma=False,
    )
```

```python
import functools
import math

import jax
import jax.numpy as jnp
from jax import lax
from jax.experimental import pallas as pl
from jax.experimental.pallas import tpu as pltpu
from jax.sharding import Mesh, PartitionSpec as P

HEAD = 128
GROUP = 6
SPAN = 128
ANS = 128
SENT_DEV = 16
SENT_OWN = 24
NX = 4
NZ = 16
N_CONTEXT = NX * NZ
N_TENSOR = 8
PIECES = 2 * N_CONTEXT
TOK_DEV = 2 * SPAN
HEADS = GROUP * N_TENSOR
S_TOT = 1024
KEYS_HALF = NZ * SPAN
SET_ROWS = GROUP * SPAN
NKM = 512
RB = 256
SLOT_PAD = 32
ANS_X = ANS // NX
TAIL = 16 + SLOT_PAD
LOW = -1e30
TINY = 1e-37
SCALE2 = math.log2(math.e) / math.sqrt(HEAD)
F32 = jnp.float32
BF16 = jnp.bfloat16

DOT_LAST = (((1,), (1,)), ((), ()))


def lanes(value):
    return jnp.broadcast_to(value, (value.shape[0], 128))


def prep_kernel(ids, len_ref, own_ref, out_ref):
    lengths = len_ref[...].astype(F32)
    owner = own_ref[...]
    before = (
        lax.broadcasted_iota(jnp.int32, (S_TOT, S_TOT), 0)
        < lax.broadcasted_iota(jnp.int32, (S_TOT, S_TOT), 1)
    ).astype(F32).astype(BF16)
    lengths = jnp.broadcast_to(lengths, (8, S_TOT))
    starts = jnp.dot(lengths.astype(BF16), before, preferred_element_type=F32)
    owned = (lax.broadcasted_iota(jnp.int32, (N_CONTEXT, S_TOT), 0) == owner).astype(F32)
    earlier = jnp.dot(owned.astype(BF16), before, preferred_element_type=F32)
    slots = jnp.sum(owned * earlier, axis=0, keepdims=True).astype(jnp.int32)
    place = jnp.where(owner % NZ == ids[1], owner // NZ * SLOT_PAD + slots, -1)
    hit = (lax.broadcasted_iota(jnp.int32, (128, S_TOT), 0) == place).astype(F32).astype(BF16)
    high = jnp.floor(starts * (1.0 / 128.0))
    low = starts - high * 128.0
    row = lax.broadcasted_iota(jnp.int32, (8, S_TOT), 0)
    parts = jnp.where(row == 0, high, jnp.where(row == 1, low, lengths))
    placed = lax.dot_general(parts.astype(BF16), hit, DOT_LAST, preferred_element_type=F32)
    start = placed[0:1] * 128.0 + placed[1:2]
    end = start + placed[2:3]
    row_out = lax.broadcasted_iota(jnp.int32, (8, 128), 0)
    out_ref[...] = jnp.where(row_out == 0, start, end).astype(jnp.int32)


def pick_kernel(ids, q_ref, *out_refs):
    my_x, my_z, start = ids[0], ids[1], ids[2]
    row = lax.broadcasted_iota(jnp.int32, (ANS_X, SPAN), 0)
    lane = lax.broadcasted_iota(jnp.int32, (ANS_X, SPAN), 1)
    piece = PIECES - 1 - (my_x * NZ + my_z)
    for j in range(NX):
        other_x = lax.rem(my_x - j + NX, NX)
        pick = (piece * SPAN + lane == start + other_x * ANS_X + row).astype(F32).astype(BF16)
        out_refs[j][...] = jnp.dot(
            pick, q_ref[SPAN:TOK_DEV, :], preferred_element_type=F32
        ).astype(BF16)


def unit(queries, keys, values, state, index, visible):
    best, total, accum = state
    width = keys.shape[0]
    for rb in range(SET_ROWS // RB):
        rows = slice(rb * RB, (rb + 1) * RB)
        raw = lax.dot_general(queries(rows), keys, DOT_LAST, preferred_element_type=F32)
        parts = [raw[:, i * 128 : (i + 1) * 128] * SCALE2 for i in range(width // 128)]
        if visible is not None:
            parts = [jnp.where(v, p, LOW) for v, p in zip(visible, parts)]
        top = functools.reduce(jnp.maximum, parts)
        old = best[index, rows, :]
        new = jnp.maximum(old, lanes(jnp.max(top, axis=1, keepdims=True)))
        alpha = jnp.exp2(old - new)
        weights = jnp.concatenate([jnp.exp2(p - new).astype(BF16) for p in parts], axis=1)
        mixed = jnp.dot(weights, values, preferred_element_type=F32)
        best[index, rows, :] = new
        total[index, rows, :] = total[index, rows, :] * alpha + mixed[:, HEAD:]
        accum[index, rows, :] = accum[index, rows, :] * alpha + mixed[:, :HEAD]


def reset(state):
    best, total, accum = state
    best[...] = jnp.full_like(best, LOW)
    total[...] = jnp.zeros_like(total)
    accum[...] = jnp.zeros_like(accum)


def limits_to_masks(limits):
    row_w = lax.broadcasted_iota(jnp.int32, (RB, 128), 0) % SPAN
    offset = lax.broadcasted_iota(jnp.int32, (RB, 128), 1) - row_w
    return [offset <= limit for limit in limits]


def pack_logs(logs):
    flipped = logs.T[0:8, :]
    hi = flipped.astype(BF16)
    rest = flipped - hi.astype(F32)
    mid = rest.astype(BF16)
    lo = (rest - mid.astype(F32)).astype(BF16)
    return jnp.concatenate([hi, mid, lo], axis=1)


def read_logs(packed):
    packed = packed.astype(F32)
    return packed[:, :128] + packed[:, 128:256] + packed[:, 256:384]


def finish(state, index, write):
    best, total, accum = state
    lane = lax.broadcasted_iota(jnp.int32, (SPAN, 128), 1)
    logs = jnp.zeros((SPAN, 128), F32)
    for h in range(GROUP):
        rows = slice(h * SPAN, (h + 1) * SPAN)
        tot = jnp.maximum(total[index, rows, :], TINY)
        logs = jnp.where(lane == h, best[index, rows, :] + jnp.log2(tot), logs)
        write(h, accum[index, rows, :] / tot)
    return pack_logs(logs)


def gather_keys(kv_ref, half, slots):
    blocks = [
        kv_ref[pl.ds(slot * TOK_DEV + pl.multiple_of(half * SPAN, SPAN), SPAN), :] for slot in slots
    ]
    ones = jnp.ones((len(blocks) * SPAN, HEAD), BF16)
    keys = jnp.concatenate([block[:, :HEAD] for block in blocks], axis=0)
    values = jnp.concatenate([block[:, HEAD:] for block in blocks], axis=0)
    return keys, jnp.concatenate([values, ones], axis=1)


def fold(state, into, index):
    best, total, accum = state
    for h in range(GROUP):
        rows = slice(h * SPAN, (h + 1) * SPAN)
        new = jnp.maximum(best[into, rows, :], best[index, rows, :])
        keep = jnp.exp2(best[into, rows, :] - new)
        add = jnp.exp2(best[index, rows, :] - new)
        total[into, rows, :] = total[into, rows, :] * keep + total[index, rows, :] * add
        accum[into, rows, :] = accum[into, rows, :] * keep + accum[index, rows, :] * add
        best[into, rows, :] = new
        best[index, rows, :] = jnp.full((SPAN, 128), LOW, F32)
        total[index, rows, :] = jnp.zeros((SPAN, 128), F32)
        accum[index, rows, :] = jnp.zeros((SPAN, HEAD), F32)


def spread(q_ref, qs):
    for half in range(2):
        for h in range(GROUP):
            qs[half, h * SPAN : (h + 1) * SPAN, :] = q_ref[
                half * SPAN : (half + 1) * SPAN, h * HEAD : (h + 1) * HEAD
            ]


def write_rows(state, msg_ref):
    for half in range(2):

        def write(h, value):
            msg_ref[half * SPAN : (half + 1) * SPAN, h * HEAD : (h + 1) * HEAD] = value.astype(BF16)

        msg_ref[TOK_DEV : TOK_DEV + 8, half * 384 : half * 384 + 384] = finish(state, half, write)


def peer_kernel(j, ids, q_ref, kv_ref, tail_ref, msg_ref, qs, *state):
    my_x = ids[0]
    upper = (lax.rem(my_x - j + NX, NX) < my_x).astype(jnp.int32)
    spread(q_ref, qs)
    reset(state)
    keys, values = gather_keys(kv_ref, 0, range(NZ))
    unit(lambda rows: qs[1, rows, :], keys, values, state, 1, None)
    keys, values = gather_keys(kv_ref, upper, range(NZ))
    unit(lambda rows: qs[upper, rows, :], keys, values, state, 0, None)

    @pl.when(upper == 1)
    def _():
        fold(state, 1, 0)

    write_rows(state, msg_ref)
    msg_ref[TOK_DEV + 8 : TOK_DEV + TAIL, :] = tail_ref[j, 8:TAIL, :]


def cited_kernel(*refs):
    ids, table = refs[0:2]
    a_refs = refs[2 : 2 + NX]
    kv_ref, tail_ref, qs, flat = refs[2 + NX : 6 + NX]
    state = refs[6 + NX :]
    my_x, start = ids[0], ids[2]
    other_x = [lax.rem(my_x - j + NX, NX) for j in range(NX)]
    for j in range(NX):
        for h in range(GROUP):
            at = pl.ds(pl.multiple_of(h * ANS + other_x[j] * ANS_X, ANS_X), ANS_X)
            qs[at, :] = a_refs[j][:, h * HEAD : (h + 1) * HEAD]
    col = lax.broadcasted_iota(jnp.int32, (SPAN, 128), 0)

    def bases(slot):
        context = my_x * NZ + slot
        return context * SPAN, (PIECES - 1 - context) * SPAN

    def tagged(half):
        keys, _ = gather_keys(kv_ref, half, range(NZ))
        tags = []
        for slot in range(NZ):
            place = bases(slot)[half] + col
            inside = jnp.logical_and(place >= table[0:1, :], place < table[1:2, :])
            tags.append(inside.astype(F32).astype(BF16))
        ones = jnp.ones((KEYS_HALF, HEAD), BF16)
        return keys, jnp.concatenate([jnp.concatenate(tags, axis=0), ones], axis=1)

    reset(state)
    keys, values = tagged(0)
    unit(lambda rows: qs[rows, :], keys, values, state, 0, None)
    keys, values = tagged(1)
    limits = [start - bases(slot)[1] for slot in range(NZ)]
    unit(lambda rows: qs[rows, :], keys, values, state, 1, limits_to_masks(limits))
    fold(state, 0, 1)

    def keep(h, value):
        flat[:, h * ANS : (h + 1) * ANS] = value.T.astype(BF16)

    logs = finish(state, 0, keep)
    for j in range(NX):
        tail_ref[j, 8:16, 0:384] = logs
        tail_ref[j, 16:TAIL, :] = flat[
            pl.ds(pl.multiple_of(other_x[j] * SLOT_PAD, SLOT_PAD), SLOT_PAD), :
        ]


def own_kernel(ids, q_ref, kv_ref, msg_ref, qs, *state):
    my_z = ids[1]
    per = NKM // SPAN
    spread(q_ref, qs)
    reset(state)
    keys, values = gather_keys(kv_ref, 0, range(NZ))
    unit(lambda rows: qs[1, rows, :], keys, values, state, 1, None)

    def masked(half, g):
        slots = [g * per + i for i in range(per)]
        limits = []
        for slot in slots:
            seen = slot < my_z if half == 0 else slot > my_z
            limits.append(jnp.where(slot == my_z, 0, jnp.where(seen, SPAN, -SPAN)))
        keys, values = gather_keys(kv_ref, half, slots)
        unit(lambda rows: qs[half, rows, :], keys, values, state, half, limits_to_masks(limits))

    def low(g, carry):
        masked(0, g)
        return carry

    def high(g, carry):
        masked(1, g)
        return carry

    lax.fori_loop(0, my_z // per + 1, low, 0)
    lax.fori_loop(my_z // per, NZ // per, high, 0)
    write_rows(state, msg_ref)


def shares_of(logs):
    top = functools.reduce(jnp.maximum, logs)
    shares = [jnp.exp2(v - top) for v in logs]
    tot = functools.reduce(jnp.add, shares)
    return [v / tot for v in shares]


def combine_kernel(*refs):
    msgs, out_ref = refs[:NX], refs[NX]
    pad = jnp.zeros((SPAN - 8, SPAN), F32)
    for half in range(2):
        logs = slice(half * 384, half * 384 + 384)
        shares = shares_of([read_logs(m[TOK_DEV : TOK_DEV + 8, logs]) for m in msgs])
        flipped = [jnp.concatenate([v, pad], axis=0).T for v in shares]
        rows = slice(half * SPAN, (half + 1) * SPAN)
        for h in range(GROUP):
            cols = slice(h * HEAD, (h + 1) * HEAD)
            pieces = [
                m[rows, cols].astype(F32) * lanes(f[:, h : h + 1]) for m, f in zip(msgs, flipped)
            ]
            out_ref[rows, cols] = functools.reduce(jnp.add, pieces).astype(BF16)


def cite_kernel(ids, tail_ref, *refs):
    msgs, cite_ref = refs[: NX - 1], refs[NX - 1]
    tails = [tail_ref.at[0]] + [m.at[TOK_DEV : TOK_DEV + TAIL] for m in msgs]
    shares = shares_of([read_logs(t[8:16, 0:384]) for t in tails])
    value = jnp.zeros((SLOT_PAD, ANS), F32)
    for tail, share in zip(tails, shares):
        for h in range(GROUP):
            block = tail[16:TAIL, h * ANS : (h + 1) * ANS].astype(F32)
            value = value + block * share[h : h + 1, :]
    row = lax.broadcasted_iota(jnp.int32, (SLOT_PAD, ANS), 1)
    factor = (ids[2] + row + 1).astype(F32) * (SENT_DEV / (TOK_DEV * HEADS))
    value = value * factor
    for t in range(N_TENSOR):
        cite_ref[t] = value[0:SENT_OWN, :]


VMEM_SPEC = pl.BlockSpec(memory_space=pltpu.VMEM)
SMEM_SPEC = pl.BlockSpec(memory_space=pltpu.SMEM)


def call(kernel, name, out_shape, scalars, arrays, scratch=(), flops=1e6, moved=1e6):
    many = isinstance(out_shape, list)
    return pl.pallas_call(
        kernel,
        out_shape=out_shape,
        in_specs=[SMEM_SPEC] * scalars + [VMEM_SPEC] * arrays,
        out_specs=[VMEM_SPEC] * len(out_shape) if many else VMEM_SPEC,
        scratch_shapes=list(scratch),
        compiler_params=pltpu.CompilerParams(vmem_limit_bytes=40 << 20),
        cost_estimate=pl.CostEstimate(
            flops=int(flops), bytes_accessed=int(moved), transcendentals=0
        ),
        name=name,
    )


def ring(count, step):
    return [(i, (i + step) % count) for i in range(count)]


def per_device(queries, key_states, value_states, sentence_lengths, sentence_owner, answer_start):
    my_x = lax.axis_index("x")
    my_z = lax.axis_index("z")
    ids = jnp.stack([my_x, my_z, answer_start[0]]).astype(jnp.int32)

    table = call(
        prep_kernel, "prep", jax.ShapeDtypeStruct((8, 128), jnp.int32), 1, 2, flops=3e8, moved=2e4
    )(ids, sentence_lengths.reshape(1, S_TOT), sentence_owner.reshape(1, S_TOT))

    pairs = lax.all_gather(
        jnp.concatenate([key_states, value_states], axis=1), "z", axis=0, tiled=True
    )
    q_all = [queries] + [lax.ppermute(queries, "x", ring(NX, j)) for j in (1, 2, 3)]
    part = jax.ShapeDtypeStruct((ANS_X, GROUP * HEAD), BF16)
    picked = call(pick_kernel, "pick", [part] * NX, 1, 1, flops=3e7)(ids, queries)
    asked = picked[0]
    for j in (1, 2, 3):
        asked = asked + lax.ppermute(picked[j], "x", ring(NX, -j))
    for shifts in ((8, 4, -4), (2, 1, -1)):
        got = [lax.ppermute(asked, "z", ring(NZ, s)) for s in shifts]
        asked = functools.reduce(jnp.add, got, asked)
    asked_all = [asked] + [lax.ppermute(asked, "x", ring(NX, j)) for j in (1, 2, 3)]

    width = GROUP * HEAD

    def state(sets):
        return [pltpu.VMEM((sets, SET_ROWS, 128), F32)] * 3

    tails = call(
        cited_kernel,
        "attend_cited",
        jax.ShapeDtypeStruct((NX, TAIL, width), BF16),
        1,
        NX + 2,
        [pltpu.VMEM((SET_ROWS, HEAD), BF16), pltpu.VMEM((128, GROUP * ANS), BF16)] + state(2),
        flops=2e9,
        moved=3e6,
    )(ids, table, *asked_all, pairs)
    got = [None] * NX
    for j in (2, 1, 3):
        msg = call(
            functools.partial(peer_kernel, j),
            "attend_peer",
            jax.ShapeDtypeStruct((TOK_DEV + TAIL, width), BF16),
            1,
            3,
            [pltpu.VMEM((2, SET_ROWS, HEAD), BF16)] + state(2),
            flops=2e9,
            moved=3e6,
        )(ids, q_all[j], pairs, tails)
        got[j] = lax.ppermute(msg, "x", ring(NX, -j))
    got[0] = call(
        own_kernel,
        "attend_own",
        jax.ShapeDtypeStruct((TOK_DEV + 16, width), BF16),
        1,
        2,
        [pltpu.VMEM((2, SET_ROWS, HEAD), BF16)] + state(2),
        flops=2e9,
        moved=3e6,
    )(ids, queries, pairs)
    got = lax.optimization_barrier(got)

    cited = call(
        cite_kernel,
        "cite",
        jax.ShapeDtypeStruct((N_TENSOR, SENT_OWN, ANS), F32),
        1,
        NX,
        flops=1e6,
        moved=1e6,
    )(ids, tails, *got[1:])
    attention = call(
        combine_kernel,
        "combine",
        jax.ShapeDtypeStruct((TOK_DEV, width), BF16),
        0,
        NX,
        flops=1e7,
        moved=3e6,
    )(*got)

    parts = jnp.sum(lax.all_to_all(cited, ("y", "core"), 0, 0), axis=0)
    share = ANS // N_TENSOR
    first = (lax.axis_index("y") * 2 + lax.axis_index("core")) * share
    citations = lax.dynamic_slice_in_dim(parts, first, share, 1)
    return (attention, citations)


def solution(mesh):
    grid = Mesh(mesh.devices.reshape(NX, 2, NX, NZ), ("y", "core", "x", "z"))
    context, tensor = ("x", "z"), ("y", "core")
    return jax.shard_map(
        per_device,
        mesh=grid,
        in_specs=(
            P(context, tensor),
            P(context, tensor),
            P(context, tensor),
            P(),
            P(),
            P(),
        ),
        out_specs=(P(context, tensor), P(context, tensor)),
        check_vma=False,
    )
```

```python
import functools
import math

import jax
import jax.numpy as jnp
from jax import lax
from jax.experimental import pallas as pl
from jax.experimental.pallas import tpu as pltpu
from jax.sharding import Mesh, PartitionSpec as P

HEAD = 128
GROUP = 6
SPAN = 128
ANS = 128
SENT_DEV = 16
SENT_OWN = 24
NX = 4
NZ = 16
N_CONTEXT = NX * NZ
N_TENSOR = 8
PIECES = 2 * N_CONTEXT
TOK_DEV = 2 * SPAN
HEADS = GROUP * N_TENSOR
S_TOT = 1024
KEYS_HALF = NZ * SPAN
SET_ROWS = GROUP * SPAN
RB = 256
SLOT_PAD = 32
ANS_X = ANS // NX
TAIL = 16 + SLOT_PAD
LOW = -1e30
TINY = 1e-37
SCALE2 = math.log2(math.e) / math.sqrt(HEAD)
F32 = jnp.float32
BF16 = jnp.bfloat16

DOT_LAST = (((1,), (1,)), ((), ()))


def lanes(value):
    return jnp.broadcast_to(value, (value.shape[0], 128))


def prep_kernel(ids, len_ref, own_ref, out_ref):
    lengths = len_ref[...].astype(F32)
    owner = own_ref[...]
    before = (
        lax.broadcasted_iota(jnp.int32, (S_TOT, S_TOT), 0)
        < lax.broadcasted_iota(jnp.int32, (S_TOT, S_TOT), 1)
    ).astype(F32).astype(BF16)
    lengths = jnp.broadcast_to(lengths, (8, S_TOT))
    starts = jnp.dot(lengths.astype(BF16), before, preferred_element_type=F32)
    owned = (lax.broadcasted_iota(jnp.int32, (N_CONTEXT, S_TOT), 0) == owner).astype(F32)
    earlier = jnp.dot(owned.astype(BF16), before, preferred_element_type=F32)
    slots = jnp.sum(owned * earlier, axis=0, keepdims=True).astype(jnp.int32)
    place = jnp.where(owner % NZ == ids[1], owner // NZ * SLOT_PAD + slots, -1)
    hit = (lax.broadcasted_iota(jnp.int32, (128, S_TOT), 0) == place).astype(F32).astype(BF16)
    high = jnp.floor(starts * (1.0 / 128.0))
    low = starts - high * 128.0
    row = lax.broadcasted_iota(jnp.int32, (8, S_TOT), 0)
    parts = jnp.where(row == 0, high, jnp.where(row == 1, low, lengths))
    placed = lax.dot_general(parts.astype(BF16), hit, DOT_LAST, preferred_element_type=F32)
    start = placed[0:1] * 128.0 + placed[1:2]
    end = start + placed[2:3]
    row_out = lax.broadcasted_iota(jnp.int32, (8, 128), 0)
    out_ref[...] = jnp.where(row_out == 0, start, end).astype(jnp.int32)


def pick_kernel(ids, q_ref, *out_refs):
    my_x, my_z, start = ids[0], ids[1], ids[2]
    row = lax.broadcasted_iota(jnp.int32, (ANS_X, SPAN), 0)
    lane = lax.broadcasted_iota(jnp.int32, (ANS_X, SPAN), 1)
    piece = PIECES - 1 - (my_x * NZ + my_z)
    for j in range(NX):
        other_x = lax.rem(my_x - j + NX, NX)
        pick = (piece * SPAN + lane == start + other_x * ANS_X + row).astype(F32).astype(BF16)
        out_refs[j][...] = jnp.dot(
            pick, q_ref[SPAN:TOK_DEV, :], preferred_element_type=F32
        ).astype(BF16)


def unit(queries, keys, values, state, index, visible):
    best, total, accum = state
    width = keys.shape[0]
    for rb in range(SET_ROWS // RB):
        rows = slice(rb * RB, (rb + 1) * RB)
        raw = lax.dot_general(queries(rows), keys, DOT_LAST, preferred_element_type=F32)
        parts = [raw[:, i * 128 : (i + 1) * 128] for i in range(width // 128)]
        if visible is not None:
            parts = [jnp.where(v, p, LOW) for v, p in zip(visible, parts)]
        top = functools.reduce(jnp.maximum, parts)
        old = best[index, rows, :]
        new = jnp.maximum(old, lanes(jnp.max(top, axis=1, keepdims=True)))
        alpha = jnp.exp2((old - new) * SCALE2)
        weights = [jnp.exp2((p - new) * SCALE2).astype(BF16) for p in parts]
        weights = jnp.concatenate(weights, axis=1)
        mixed = jnp.dot(weights, values, preferred_element_type=F32)
        best[index, rows, :] = new
        total[index, rows, :] = total[index, rows, :] * alpha + mixed[:, HEAD:]
        accum[index, rows, :] = accum[index, rows, :] * alpha + mixed[:, :HEAD]


def reset(state):
    best, total, accum = state
    best[...] = jnp.full_like(best, LOW)
    total[...] = jnp.zeros_like(total)
    accum[...] = jnp.zeros_like(accum)


def limits_to_masks(limits):
    row_w = lax.broadcasted_iota(jnp.int32, (RB, 128), 0) % SPAN
    offset = lax.broadcasted_iota(jnp.int32, (RB, 128), 1) - row_w
    return [offset <= limit for limit in limits]


def pack_logs(logs):
    flipped = logs.T[0:8, :]
    hi = flipped.astype(BF16)
    rest = flipped - hi.astype(F32)
    mid = rest.astype(BF16)
    lo = (rest - mid.astype(F32)).astype(BF16)
    return jnp.concatenate([hi, mid, lo], axis=1)


def read_logs(packed):
    packed = packed.astype(F32)
    return packed[:, :128] + packed[:, 128:256] + packed[:, 256:384]


def finish(state, index, write):
    best, total, accum = state
    lane = lax.broadcasted_iota(jnp.int32, (SPAN, 128), 1)
    logs = jnp.zeros((SPAN, 128), F32)
    for h in range(GROUP):
        rows = slice(h * SPAN, (h + 1) * SPAN)
        tot = jnp.maximum(total[index, rows, :], TINY)
        logs = jnp.where(lane == h, best[index, rows, :] * SCALE2 + jnp.log2(tot), logs)
        write(h, accum[index, rows, :] / tot)
    return pack_logs(logs)


def gather_keys(kv_ref, half, slots):
    blocks = [
        kv_ref[pl.ds(slot * TOK_DEV + pl.multiple_of(half * SPAN, SPAN), SPAN), :] for slot in slots
    ]
    ones = jnp.ones((len(blocks) * SPAN, HEAD), BF16)
    keys = jnp.concatenate([block[:, :HEAD] for block in blocks], axis=0)
    values = jnp.concatenate([block[:, HEAD:] for block in blocks], axis=0)
    return keys, jnp.concatenate([values, ones], axis=1)


def fold(state, into, index):
    best, total, accum = state
    for h in range(GROUP):
        rows = slice(h * SPAN, (h + 1) * SPAN)
        new = jnp.maximum(best[into, rows, :], best[index, rows, :])
        keep = jnp.exp2((best[into, rows, :] - new) * SCALE2)
        add = jnp.exp2((best[index, rows, :] - new) * SCALE2)
        total[into, rows, :] = total[into, rows, :] * keep + total[index, rows, :] * add
        accum[into, rows, :] = accum[into, rows, :] * keep + accum[index, rows, :] * add
        best[into, rows, :] = new
        best[index, rows, :] = jnp.full((SPAN, 128), LOW, F32)
        total[index, rows, :] = jnp.zeros((SPAN, 128), F32)
        accum[index, rows, :] = jnp.zeros((SPAN, HEAD), F32)


def spread(q_ref, qs):
    for half in range(2):
        for h in range(GROUP):
            qs[half, h * SPAN : (h + 1) * SPAN, :] = q_ref[
                half * SPAN : (half + 1) * SPAN, h * HEAD : (h + 1) * HEAD
            ]


def write_rows(state, msg_ref, base=0):
    for half in range(2):

        def write(h, value):
            msg_ref[half * SPAN : (half + 1) * SPAN, h * HEAD : (h + 1) * HEAD] = value.astype(BF16)

        msg_ref[TOK_DEV : TOK_DEV + 8, half * 384 : half * 384 + 384] = finish(
            state, base + half, write
        )


def peers_kernel(peers, *refs):
    count = len(peers)
    ids = refs[0]
    q_refs = refs[1 : 1 + count]
    kv_ref, tail_ref = refs[1 + count : 3 + count]
    msg_refs = refs[3 + count : 3 + 2 * count]
    qs = refs[3 + 2 * count]
    state = refs[4 + 2 * count :]
    my_x = ids[0]
    for i in range(count):
        spread(q_refs[i], qs.at[i])
    reset(state)

    def step(i, carry):
        j = peers[0] + i * (peers[-1] - peers[0])
        upper = (lax.rem(my_x - j + NX, NX) < my_x).astype(jnp.int32)
        keys, values = gather_keys(kv_ref, 0, range(NZ))
        unit(lambda rows: qs[i, 1, rows, :], keys, values, state, 2 * i + 1, None)
        keys, values = gather_keys(kv_ref, upper, range(NZ))
        unit(lambda rows: qs[i, upper, rows, :], keys, values, state, 2 * i, None)

        @pl.when(upper == 1)
        def _():
            fold(state, 2 * i + 1, 2 * i)

        return carry

    lax.fori_loop(0, count, step, 0)
    for i, j in enumerate(peers):
        write_rows(state, msg_refs[i], 2 * i)
        msg_refs[i][TOK_DEV + 8 : TOK_DEV + TAIL, :] = tail_ref[j, 8:TAIL, :]


def cited_kernel(*refs):
    ids, table = refs[0:2]
    a_refs = refs[2 : 2 + NX]
    kv_ref, tail_ref, qs, flat = refs[2 + NX : 6 + NX]
    state = refs[6 + NX :]
    my_x, start = ids[0], ids[2]
    other_x = [lax.rem(my_x - j + NX, NX) for j in range(NX)]
    for j in range(NX):
        for h in range(GROUP):
            at = pl.ds(pl.multiple_of(h * ANS + other_x[j] * ANS_X, ANS_X), ANS_X)
            qs[at, :] = a_refs[j][:, h * HEAD : (h + 1) * HEAD]
    col = lax.broadcasted_iota(jnp.int32, (SPAN, 128), 0)

    def bases(slot):
        context = my_x * NZ + slot
        return context * SPAN, (PIECES - 1 - context) * SPAN

    def tagged(half):
        keys, _ = gather_keys(kv_ref, half, range(NZ))
        tags = []
        for slot in range(NZ):
            place = bases(slot)[half] + col
            inside = jnp.logical_and(place >= table[0:1, :], place < table[1:2, :])
            tags.append(inside.astype(F32).astype(BF16))
        ones = jnp.ones((KEYS_HALF, HEAD), BF16)
        return keys, jnp.concatenate([jnp.concatenate(tags, axis=0), ones], axis=1)

    reset(state)
    keys, values = tagged(0)
    unit(lambda rows: qs[rows, :], keys, values, state, 0, None)
    keys, values = tagged(1)
    limits = [start - bases(slot)[1] for slot in range(NZ)]
    unit(lambda rows: qs[rows, :], keys, values, state, 1, limits_to_masks(limits))
    fold(state, 0, 1)

    def keep(h, value):
        flat[:, h * ANS : (h + 1) * ANS] = value.T.astype(BF16)

    logs = finish(state, 0, keep)
    for j in range(NX):
        tail_ref[j, 8:16, 0:384] = logs
        tail_ref[j, 16:TAIL, :] = flat[
            pl.ds(pl.multiple_of(other_x[j] * SLOT_PAD, SLOT_PAD), SLOT_PAD), :
        ]


def own_kernel(ids, q_ref, kv_ref, msg_ref, qs, *state):
    my_z = ids[1]
    per = NZ // 2
    spread(q_ref, qs)
    reset(state)
    keys, values = gather_keys(kv_ref, 0, range(NZ))
    unit(lambda rows: qs[1, rows, :], keys, values, state, 1, None)

    late = (my_z >= per).astype(jnp.int32)
    plain = 1 - late
    slots = [plain * per + i for i in range(per)]
    keys, values = gather_keys(kv_ref, plain, slots)
    unit(lambda rows: qs[plain, rows, :], keys, values, state, 2, None)

    slots = [late * per + i for i in range(per)]
    for half in range(2):
        limits = []
        for slot in slots:
            seen = slot < my_z if half == 0 else slot > my_z
            limits.append(jnp.where(slot == my_z, 0, jnp.where(seen, SPAN, -SPAN)))
        keys, values = gather_keys(kv_ref, half, slots)
        into = 0 if half == 0 else 3
        unit(lambda rows: qs[half, rows, :], keys, values, state, into, limits_to_masks(limits))
    fold(state, 1, 3)
    fold(state, plain, 2)
    write_rows(state, msg_ref)


def shares_of(logs):
    top = functools.reduce(jnp.maximum, logs)
    shares = [jnp.exp2(v - top) for v in logs]
    tot = functools.reduce(jnp.add, shares)
    return [v / tot for v in shares]


def combine_kernel(*refs):
    msgs, out_ref = refs[:NX], refs[NX]
    pad = jnp.zeros((SPAN - 8, SPAN), F32)
    for half in range(2):
        logs = slice(half * 384, half * 384 + 384)
        shares = shares_of([read_logs(m[TOK_DEV : TOK_DEV + 8, logs]) for m in msgs])
        flipped = [jnp.concatenate([v, pad], axis=0).T for v in shares]
        rows = slice(half * SPAN, (half + 1) * SPAN)
        for h in range(GROUP):
            cols = slice(h * HEAD, (h + 1) * HEAD)
            pieces = [
                m[rows, cols].astype(F32) * lanes(f[:, h : h + 1]) for m, f in zip(msgs, flipped)
            ]
            out_ref[rows, cols] = functools.reduce(jnp.add, pieces).astype(BF16)


def cite_kernel(ids, tail_ref, *refs):
    msgs, cite_ref = refs[: NX - 1], refs[NX - 1]
    tails = [tail_ref.at[0]] + [m.at[TOK_DEV : TOK_DEV + TAIL] for m in msgs]
    shares = shares_of([read_logs(t[8:16, 0:384]) for t in tails])
    value = jnp.zeros((SLOT_PAD, ANS), F32)
    for tail, share in zip(tails, shares):
        for h in range(GROUP):
            block = tail[16:TAIL, h * ANS : (h + 1) * ANS].astype(F32)
            value = value + block * share[h : h + 1, :]
    row = lax.broadcasted_iota(jnp.int32, (SLOT_PAD, ANS), 1)
    factor = (ids[2] + row + 1).astype(F32) * (SENT_DEV / (TOK_DEV * HEADS))
    value = value * factor
    for t in range(N_TENSOR):
        cite_ref[t] = value[0:SENT_OWN, :]


VMEM_SPEC = pl.BlockSpec(memory_space=pltpu.VMEM)
SMEM_SPEC = pl.BlockSpec(memory_space=pltpu.SMEM)


def call(kernel, name, out_shape, scalars, arrays, scratch=(), flops=1e6, moved=1e6):
    many = isinstance(out_shape, list)
    return pl.pallas_call(
        kernel,
        out_shape=out_shape,
        in_specs=[SMEM_SPEC] * scalars + [VMEM_SPEC] * arrays,
        out_specs=[VMEM_SPEC] * len(out_shape) if many else VMEM_SPEC,
        scratch_shapes=list(scratch),
        compiler_params=pltpu.CompilerParams(vmem_limit_bytes=40 << 20),
        cost_estimate=pl.CostEstimate(
            flops=int(flops), bytes_accessed=int(moved), transcendentals=0
        ),
        name=name,
    )


def ring(count, step):
    return [(i, (i + step) % count) for i in range(count)]


def per_device(queries, key_states, value_states, sentence_lengths, sentence_owner, answer_start):
    my_x = lax.axis_index("x")
    my_z = lax.axis_index("z")
    ids = jnp.stack([my_x, my_z, answer_start[0]]).astype(jnp.int32)

    table = call(
        prep_kernel, "prep", jax.ShapeDtypeStruct((8, 128), jnp.int32), 1, 2, flops=3e8, moved=2e4
    )(ids, sentence_lengths.reshape(1, S_TOT), sentence_owner.reshape(1, S_TOT))

    pairs = lax.all_gather(
        jnp.concatenate([key_states, value_states], axis=1), "z", axis=0, tiled=True
    )
    q_all = [queries] + [lax.ppermute(queries, "x", ring(NX, j)) for j in (1, 2, 3)]
    part = jax.ShapeDtypeStruct((ANS_X, GROUP * HEAD), BF16)
    picked = call(pick_kernel, "pick", [part] * NX, 1, 1, flops=3e7)(ids, queries)
    asked = picked[0]
    for j in (1, 2, 3):
        asked = asked + lax.ppermute(picked[j], "x", ring(NX, -j))
    for shifts in ((8, 4, -4), (2, 1, -1)):
        got = [lax.ppermute(asked, "z", ring(NZ, s)) for s in shifts]
        asked = functools.reduce(jnp.add, got, asked)
    asked_all = [asked] + [lax.ppermute(asked, "x", ring(NX, j)) for j in (1, 2, 3)]

    width = GROUP * HEAD

    def state(sets):
        return [pltpu.VMEM((sets, SET_ROWS, 128), F32)] * 3

    tails = call(
        cited_kernel,
        "attend_cited",
        jax.ShapeDtypeStruct((NX, TAIL, width), BF16),
        1,
        NX + 2,
        [pltpu.VMEM((SET_ROWS, HEAD), BF16), pltpu.VMEM((128, GROUP * ANS), BF16)] + state(2),
        flops=2e9,
        moved=3e6,
    )(ids, table, *asked_all, pairs)
    got = [None] * NX
    for peers in ((2,), (1, 3)):
        msgs = call(
            functools.partial(peers_kernel, peers),
            "attend_peers",
            [jax.ShapeDtypeStruct((TOK_DEV + TAIL, width), BF16)] * len(peers),
            1,
            len(peers) + 2,
            [pltpu.VMEM((len(peers), 2, SET_ROWS, HEAD), BF16)] + state(2 * len(peers)),
            flops=2e9 * len(peers),
            moved=3e6,
        )(ids, *[q_all[j] for j in peers], pairs, tails)
        for j, msg in zip(peers, msgs):
            got[j] = lax.ppermute(msg, "x", ring(NX, -j))
    got[0] = call(
        own_kernel,
        "attend_own",
        jax.ShapeDtypeStruct((TOK_DEV + 16, width), BF16),
        1,
        2,
        [pltpu.VMEM((2, SET_ROWS, HEAD), BF16)] + state(4),
        flops=2e9,
        moved=3e6,
    )(ids, queries, pairs)
    got = lax.optimization_barrier(got)

    cited = call(
        cite_kernel,
        "cite",
        jax.ShapeDtypeStruct((N_TENSOR, SENT_OWN, ANS), F32),
        1,
        NX,
        flops=1e6,
        moved=1e6,
    )(ids, tails, *got[1:])
    attention = call(
        combine_kernel,
        "combine",
        jax.ShapeDtypeStruct((TOK_DEV, width), BF16),
        0,
        NX,
        flops=1e7,
        moved=3e6,
    )(*got)

    parts = jnp.sum(lax.all_to_all(cited, ("y", "core"), 0, 0), axis=0)
    share = ANS // N_TENSOR
    first = (lax.axis_index("y") * 2 + lax.axis_index("core")) * share
    citations = lax.dynamic_slice_in_dim(parts, first, share, 1)
    return (attention, citations)


def solution(mesh):
    grid = Mesh(mesh.devices.reshape(NX, 2, NX, NZ), ("y", "core", "x", "z"))
    context, tensor = ("x", "z"), ("y", "core")
    return jax.shard_map(
        per_device,
        mesh=grid,
        in_specs=(
            P(context, tensor),
            P(context, tensor),
            P(context, tensor),
            P(),
            P(),
            P(),
        ),
        out_specs=(P(context, tensor), P(context, tensor)),
        check_vma=False,
    )
```

```python
import functools
import math

import jax
import jax.numpy as jnp
from jax import lax
from jax.experimental import pallas as pl
from jax.experimental.pallas import tpu as pltpu
from jax.sharding import Mesh, PartitionSpec as P

HEAD = 128
GROUP = 6
SPAN = 128
ANS = 128
SENT_DEV = 16
SENT_OWN = 24
NX = 4
NZ = 16
N_CONTEXT = NX * NZ
N_TENSOR = 8
PIECES = 2 * N_CONTEXT
TOK_DEV = 2 * SPAN
HEADS = GROUP * N_TENSOR
S_TOT = 1024
KEYS_HALF = NZ * SPAN
SET_ROWS = GROUP * SPAN
RB = 256
SLOT_PAD = 32
ANS_X = ANS // NX
TAIL = 16 + SLOT_PAD
LOW = -1e30
TINY = 1e-37
SCALE2 = math.log2(math.e) / math.sqrt(HEAD)
F32 = jnp.float32
BF16 = jnp.bfloat16

DOT_LAST = (((1,), (1,)), ((), ()))


def lanes(value):
    return jnp.broadcast_to(value, (value.shape[0], 128))


def prep_kernel(ids, len_ref, own_ref, out_ref):
    lengths = len_ref[...].astype(F32)
    owner = own_ref[...]
    before = (
        lax.broadcasted_iota(jnp.int32, (S_TOT, S_TOT), 0)
        < lax.broadcasted_iota(jnp.int32, (S_TOT, S_TOT), 1)
    ).astype(F32).astype(BF16)
    lengths = jnp.broadcast_to(lengths, (8, S_TOT))
    starts = jnp.dot(lengths.astype(BF16), before, preferred_element_type=F32)
    owned = (lax.broadcasted_iota(jnp.int32, (N_CONTEXT, S_TOT), 0) == owner).astype(F32)
    earlier = jnp.dot(owned.astype(BF16), before, preferred_element_type=F32)
    slots = jnp.sum(owned * earlier, axis=0, keepdims=True).astype(jnp.int32)
    place = jnp.where(owner % NZ == ids[1], owner // NZ * SLOT_PAD + slots, -1)
    hit = (lax.broadcasted_iota(jnp.int32, (128, S_TOT), 0) == place).astype(F32).astype(BF16)
    high = jnp.floor(starts * (1.0 / 128.0))
    low = starts - high * 128.0
    row = lax.broadcasted_iota(jnp.int32, (8, S_TOT), 0)
    parts = jnp.where(row == 0, high, jnp.where(row == 1, low, lengths))
    placed = lax.dot_general(parts.astype(BF16), hit, DOT_LAST, preferred_element_type=F32)
    start = placed[0:1] * 128.0 + placed[1:2]
    end = start + placed[2:3]
    row_out = lax.broadcasted_iota(jnp.int32, (8, 128), 0)
    out_ref[...] = jnp.where(row_out == 0, start, end).astype(jnp.int32)


def pick_kernel(ids, q_ref, *out_refs):
    my_x, my_z, start = ids[0], ids[1], ids[2]
    row = lax.broadcasted_iota(jnp.int32, (ANS_X, SPAN), 0)
    lane = lax.broadcasted_iota(jnp.int32, (ANS_X, SPAN), 1)
    piece = PIECES - 1 - (my_x * NZ + my_z)
    for j in range(NX):
        other_x = lax.rem(my_x - j + NX, NX)
        pick = (piece * SPAN + lane == start + other_x * ANS_X + row).astype(F32).astype(BF16)
        out_refs[j][...] = jnp.dot(
            pick, q_ref[SPAN:TOK_DEV, :], preferred_element_type=F32
        ).astype(BF16)


def unit(queries, keys, values, state, index, visible):
    best, total, accum = state
    width = keys.shape[0]
    for rb in range(SET_ROWS // RB):
        rows = slice(rb * RB, (rb + 1) * RB)
        raw = lax.dot_general(queries(rows), keys, DOT_LAST, preferred_element_type=F32)
        parts = [raw[:, i * 128 : (i + 1) * 128] for i in range(width // 128)]
        if visible is not None:
            parts = [jnp.where(v, p, LOW) for v, p in zip(visible, parts)]
        top = functools.reduce(jnp.maximum, parts)
        old = best[index, rows, :]
        new = jnp.maximum(old, lanes(jnp.max(top, axis=1, keepdims=True)))
        alpha = jnp.exp2((old - new) * SCALE2)
        weights = [jnp.exp2((p - new) * SCALE2).astype(BF16) for p in parts]
        weights = jnp.concatenate(weights, axis=1)
        mixed = jnp.dot(weights, values, preferred_element_type=F32)
        best[index, rows, :] = new
        total[index, rows, :] = total[index, rows, :] * alpha + mixed[:, HEAD:]
        accum[index, rows, :] = accum[index, rows, :] * alpha + mixed[:, :HEAD]


def reset(state):
    best, total, accum = state
    best[...] = jnp.full_like(best, LOW)
    total[...] = jnp.zeros_like(total)
    accum[...] = jnp.zeros_like(accum)


def limits_to_masks(limits):
    row_w = lax.broadcasted_iota(jnp.int32, (RB, 128), 0) % SPAN
    offset = lax.broadcasted_iota(jnp.int32, (RB, 128), 1) - row_w
    return [offset <= limit for limit in limits]


def pack_logs(logs):
    flipped = logs.T[0:8, :]
    hi = flipped.astype(BF16)
    rest = flipped - hi.astype(F32)
    mid = rest.astype(BF16)
    lo = (rest - mid.astype(F32)).astype(BF16)
    return jnp.concatenate([hi, mid, lo], axis=1)


def read_logs(packed):
    packed = packed.astype(F32)
    return packed[:, :128] + packed[:, 128:256] + packed[:, 256:384]


def finish(state, index, write):
    best, total, accum = state
    lane = lax.broadcasted_iota(jnp.int32, (SPAN, 128), 1)
    logs = jnp.zeros((SPAN, 128), F32)
    for h in range(GROUP):
        rows = slice(h * SPAN, (h + 1) * SPAN)
        tot = jnp.maximum(total[index, rows, :], TINY)
        logs = jnp.where(lane == h, best[index, rows, :] * SCALE2 + jnp.log2(tot), logs)
        write(h, accum[index, rows, :] / tot)
    return pack_logs(logs)


def gather_keys(kv_ref, half, slots):
    blocks = [
        kv_ref[pl.ds(slot * TOK_DEV + pl.multiple_of(half * SPAN, SPAN), SPAN), :] for slot in slots
    ]
    ones = jnp.ones((len(blocks) * SPAN, HEAD), BF16)
    keys = jnp.concatenate([block[:, :HEAD] for block in blocks], axis=0)
    values = jnp.concatenate([block[:, HEAD:] for block in blocks], axis=0)
    return keys, jnp.concatenate([values, ones], axis=1)


def fold(state, into, index):
    best, total, accum = state
    for h in range(GROUP):
        rows = slice(h * SPAN, (h + 1) * SPAN)
        new = jnp.maximum(best[into, rows, :], best[index, rows, :])
        keep = jnp.exp2((best[into, rows, :] - new) * SCALE2)
        add = jnp.exp2((best[index, rows, :] - new) * SCALE2)
        total[into, rows, :] = total[into, rows, :] * keep + total[index, rows, :] * add
        accum[into, rows, :] = accum[into, rows, :] * keep + accum[index, rows, :] * add
        best[into, rows, :] = new
        best[index, rows, :] = jnp.full((SPAN, 128), LOW, F32)
        total[index, rows, :] = jnp.zeros((SPAN, 128), F32)
        accum[index, rows, :] = jnp.zeros((SPAN, HEAD), F32)


def spread(q_ref, qs):
    for half in range(2):
        for h in range(GROUP):
            qs[half, h * SPAN : (h + 1) * SPAN, :] = q_ref[
                half * SPAN : (half + 1) * SPAN, h * HEAD : (h + 1) * HEAD
            ]


def write_rows(state, msg_ref, base=0):
    for half in range(2):

        def write(h, value):
            msg_ref[half * SPAN : (half + 1) * SPAN, h * HEAD : (h + 1) * HEAD] = value.astype(BF16)

        msg_ref[TOK_DEV : TOK_DEV + 8, half * 384 : half * 384 + 384] = finish(
            state, base + half, write
        )


def peers_kernel(peers, *refs):
    count = len(peers)
    ids = refs[0]
    q_refs = refs[1 : 1 + count]
    kv_ref, tail_ref = refs[1 + count : 3 + count]
    msg_refs = refs[3 + count : 3 + 2 * count]
    qs = refs[3 + 2 * count]
    state = refs[4 + 2 * count :]
    my_x = ids[0]
    for i in range(count):
        spread(q_refs[i], qs.at[i])
    reset(state)

    def step(i, carry):
        j = peers[0] + i * (peers[-1] - peers[0])
        upper = (lax.rem(my_x - j + NX, NX) < my_x).astype(jnp.int32)
        keys, values = gather_keys(kv_ref, 0, range(NZ))
        unit(lambda rows: qs[i, 1, rows, :], keys, values, state, 2 * i + 1, None)
        keys, values = gather_keys(kv_ref, upper, range(NZ))
        unit(lambda rows: qs[i, upper, rows, :], keys, values, state, 2 * i, None)

        @pl.when(upper == 1)
        def _():
            fold(state, 2 * i + 1, 2 * i)

        return carry

    lax.fori_loop(0, count, step, 0)
    for i, j in enumerate(peers):
        write_rows(state, msg_refs[i], 2 * i)
        msg_refs[i][TOK_DEV + 8 : TOK_DEV + TAIL, :] = tail_ref[j, 8:TAIL, :]


def cited_kernel(*refs):
    ids, table = refs[0:2]
    a_refs = refs[2 : 2 + NX]
    kv_ref, tail_ref, qs, flat = refs[2 + NX : 6 + NX]
    state = refs[6 + NX :]
    my_x, start = ids[0], ids[2]
    other_x = [lax.rem(my_x - j + NX, NX) for j in range(NX)]
    for j in range(NX):
        for h in range(GROUP):
            at = pl.ds(pl.multiple_of(h * ANS + other_x[j] * ANS_X, ANS_X), ANS_X)
            qs[at, :] = a_refs[j][:, h * HEAD : (h + 1) * HEAD]
    col = lax.broadcasted_iota(jnp.int32, (SPAN, 128), 0)

    def bases(slot):
        context = my_x * NZ + slot
        return context * SPAN, (PIECES - 1 - context) * SPAN

    def tagged(half):
        keys, _ = gather_keys(kv_ref, half, range(NZ))
        tags = []
        for slot in range(NZ):
            place = bases(slot)[half] + col
            inside = jnp.logical_and(place >= table[0:1, :], place < table[1:2, :])
            tags.append(inside.astype(F32).astype(BF16))
        ones = jnp.ones((KEYS_HALF, HEAD), BF16)
        return keys, jnp.concatenate([jnp.concatenate(tags, axis=0), ones], axis=1)

    reset(state)
    keys, values = tagged(0)
    unit(lambda rows: qs[rows, :], keys, values, state, 0, None)
    keys, values = tagged(1)
    limits = [start - bases(slot)[1] for slot in range(NZ)]
    unit(lambda rows: qs[rows, :], keys, values, state, 1, limits_to_masks(limits))
    fold(state, 0, 1)

    def keep(h, value):
        flat[:, h * ANS : (h + 1) * ANS] = value.T.astype(BF16)

    logs = finish(state, 0, keep)
    for j in range(NX):
        tail_ref[j, 8:16, 0:384] = logs
        tail_ref[j, 16:TAIL, :] = flat[
            pl.ds(pl.multiple_of(other_x[j] * SLOT_PAD, SLOT_PAD), SLOT_PAD), :
        ]


def own_kernel(ids, q_ref, kv_ref, msg_ref, qs, *state):
    my_z = ids[1]
    per = NZ // 2
    spread(q_ref, qs)
    reset(state)
    keys, values = gather_keys(kv_ref, 0, range(NZ))
    unit(lambda rows: qs[1, rows, :], keys, values, state, 1, None)

    late = (my_z >= per).astype(jnp.int32)
    plain = 1 - late
    slots = [plain * per + i for i in range(per)]
    keys, values = gather_keys(kv_ref, plain, slots)
    unit(lambda rows: qs[plain, rows, :], keys, values, state, 2, None)

    slots = [late * per + i for i in range(per)]
    for half in range(2):
        limits = []
        for slot in slots:
            seen = slot < my_z if half == 0 else slot > my_z
            limits.append(jnp.where(slot == my_z, 0, jnp.where(seen, SPAN, -SPAN)))
        keys, values = gather_keys(kv_ref, half, slots)
        into = 0 if half == 0 else 3
        unit(lambda rows: qs[half, rows, :], keys, values, state, into, limits_to_masks(limits))
    fold(state, 1, 3)
    fold(state, plain, 2)
    write_rows(state, msg_ref)


def shares_of(logs):
    top = functools.reduce(jnp.maximum, logs)
    shares = [jnp.exp2(v - top) for v in logs]
    tot = functools.reduce(jnp.add, shares)
    return [v / tot for v in shares]


def combine_kernel(*refs):
    msgs, out_ref = refs[:NX], refs[NX]
    pad = jnp.zeros((SPAN - 8, SPAN), F32)
    for half in range(2):
        logs = slice(half * 384, half * 384 + 384)
        shares = shares_of([read_logs(m[TOK_DEV : TOK_DEV + 8, logs]) for m in msgs])
        flipped = [jnp.concatenate([v, pad], axis=0).T for v in shares]
        rows = slice(half * SPAN, (half + 1) * SPAN)
        for h in range(GROUP):
            cols = slice(h * HEAD, (h + 1) * HEAD)
            pieces = [
                m[rows, cols].astype(F32) * lanes(f[:, h : h + 1]) for m, f in zip(msgs, flipped)
            ]
            out_ref[rows, cols] = functools.reduce(jnp.add, pieces).astype(BF16)


def cite_kernel(ids, tail_ref, *refs):
    msgs, cite_ref = refs[: NX - 1], refs[NX - 1]
    tails = [tail_ref.at[0]] + [m.at[TOK_DEV : TOK_DEV + TAIL] for m in msgs]
    shares = shares_of([read_logs(t[8:16, 0:384]) for t in tails])
    value = jnp.zeros((SLOT_PAD, ANS), F32)
    for tail, share in zip(tails, shares):
        for h in range(GROUP):
            block = tail[16:TAIL, h * ANS : (h + 1) * ANS].astype(F32)
            value = value + block * share[h : h + 1, :]
    row = lax.broadcasted_iota(jnp.int32, (SLOT_PAD, ANS), 1)
    factor = (ids[2] + row + 1).astype(F32) * (SENT_DEV / (TOK_DEV * HEADS))
    value = value * factor
    rest = jnp.zeros((ANS - SLOT_PAD, ANS), F32)
    flipped = jnp.concatenate([value, rest], axis=0).T
    share = ANS // N_TENSOR
    for t in range(N_TENSOR):
        cite_ref[t] = flipped[t * share : (t + 1) * share, :]


VMEM_SPEC = pl.BlockSpec(memory_space=pltpu.VMEM)
SMEM_SPEC = pl.BlockSpec(memory_space=pltpu.SMEM)


def call(kernel, name, out_shape, scalars, arrays, scratch=(), flops=1e6, moved=1e6):
    many = isinstance(out_shape, list)
    return pl.pallas_call(
        kernel,
        out_shape=out_shape,
        in_specs=[SMEM_SPEC] * scalars + [VMEM_SPEC] * arrays,
        out_specs=[VMEM_SPEC] * len(out_shape) if many else VMEM_SPEC,
        scratch_shapes=list(scratch),
        compiler_params=pltpu.CompilerParams(vmem_limit_bytes=40 << 20),
        cost_estimate=pl.CostEstimate(
            flops=int(flops), bytes_accessed=int(moved), transcendentals=0
        ),
        name=name,
    )


def ring(count, step):
    return [(i, (i + step) % count) for i in range(count)]


def per_device(queries, key_states, value_states, sentence_lengths, sentence_owner, answer_start):
    my_x = lax.axis_index("x")
    my_z = lax.axis_index("z")
    ids = jnp.stack([my_x, my_z, answer_start[0]]).astype(jnp.int32)

    table = call(
        prep_kernel, "prep", jax.ShapeDtypeStruct((8, 128), jnp.int32), 1, 2, flops=3e8, moved=2e4
    )(ids, sentence_lengths.reshape(1, S_TOT), sentence_owner.reshape(1, S_TOT))

    pairs = lax.all_gather(
        jnp.concatenate([key_states, value_states], axis=1), "z", axis=0, tiled=True
    )
    q_all = [queries] + [lax.ppermute(queries, "x", ring(NX, j)) for j in (1, 2, 3)]
    part = jax.ShapeDtypeStruct((ANS_X, GROUP * HEAD), BF16)
    picked = call(pick_kernel, "pick", [part] * NX, 1, 1, flops=3e7)(ids, queries)
    asked = picked[0]
    for j in (1, 2, 3):
        asked = asked + lax.ppermute(picked[j], "x", ring(NX, -j))
    for shifts in ((8, 4, -4), (2, 1, -1)):
        got = [lax.ppermute(asked, "z", ring(NZ, s)) for s in shifts]
        asked = functools.reduce(jnp.add, got, asked)
    asked_all = [asked] + [lax.ppermute(asked, "x", ring(NX, j)) for j in (1, 2, 3)]

    width = GROUP * HEAD

    def state(sets):
        return [pltpu.VMEM((sets, SET_ROWS, 128), F32)] * 3

    tails = call(
        cited_kernel,
        "attend_cited",
        jax.ShapeDtypeStruct((NX, TAIL, width), BF16),
        1,
        NX + 2,
        [pltpu.VMEM((SET_ROWS, HEAD), BF16), pltpu.VMEM((128, GROUP * ANS), BF16)] + state(2),
        flops=2e9,
        moved=3e6,
    )(ids, table, *asked_all, pairs)
    got = [None] * NX
    for peers in ((2,), (1, 3)):
        msgs = call(
            functools.partial(peers_kernel, peers),
            "attend_peers",
            [jax.ShapeDtypeStruct((TOK_DEV + TAIL, width), BF16)] * len(peers),
            1,
            len(peers) + 2,
            [pltpu.VMEM((len(peers), 2, SET_ROWS, HEAD), BF16)] + state(2 * len(peers)),
            flops=2e9 * len(peers),
            moved=3e6,
        )(ids, *[q_all[j] for j in peers], pairs, tails)
        for j, msg in zip(peers, msgs):
            got[j] = lax.ppermute(msg, "x", ring(NX, -j))
    got[0] = call(
        own_kernel,
        "attend_own",
        jax.ShapeDtypeStruct((TOK_DEV + 16, width), BF16),
        1,
        2,
        [pltpu.VMEM((2, SET_ROWS, HEAD), BF16)] + state(4),
        flops=2e9,
        moved=3e6,
    )(ids, queries, pairs)
    got = lax.optimization_barrier(got)

    cited = call(
        cite_kernel,
        "cite",
        jax.ShapeDtypeStruct((N_TENSOR, ANS // N_TENSOR, ANS), F32),
        1,
        NX,
        flops=1e6,
        moved=1e6,
    )(ids, tails, *got[1:])
    attention = call(
        combine_kernel,
        "combine",
        jax.ShapeDtypeStruct((TOK_DEV, width), BF16),
        0,
        NX,
        flops=1e7,
        moved=3e6,
    )(*got)

    parts = jnp.sum(lax.all_to_all(cited, ("y", "core"), 0, 0), axis=0)
    citations = parts[:, :SENT_OWN].T
    return (attention, citations)


def solution(mesh):
    grid = Mesh(mesh.devices.reshape(NX, 2, NX, NZ), ("y", "core", "x", "z"))
    context, tensor = ("x", "z"), ("y", "core")
    return jax.shard_map(
        per_device,
        mesh=grid,
        in_specs=(
            P(context, tensor),
            P(context, tensor),
            P(context, tensor),
            P(),
            P(),
            P(),
        ),
        out_specs=(P(context, tensor), P(context, tensor)),
        check_vma=False,
    )
```

```python
import functools
import math

import jax
import jax.numpy as jnp
from jax import lax
from jax.experimental import pallas as pl
from jax.experimental.pallas import tpu as pltpu
from jax.sharding import Mesh, PartitionSpec as P

HEAD = 128
GROUP = 6
SPAN = 128
ANS = 128
SENT_DEV = 16
SENT_OWN = 24
NX = 4
NZ = 16
N_CONTEXT = NX * NZ
N_TENSOR = 8
PIECES = 2 * N_CONTEXT
TOK_DEV = 2 * SPAN
HEADS = GROUP * N_TENSOR
S_TOT = 1024
KEYS_HALF = NZ * SPAN
SET_ROWS = GROUP * SPAN
RB = 128
SLOT_PAD = 32
ANS_X = ANS // NX
TAIL = 16 + SLOT_PAD
LOW = -1e30
TINY = 1e-37
SCALE2 = math.log2(math.e) / math.sqrt(HEAD)
F32 = jnp.float32
BF16 = jnp.bfloat16

DOT_LAST = (((1,), (1,)), ((), ()))


def lanes(value):
    return jnp.broadcast_to(value, (value.shape[0], 128))


def prep_kernel(ids, len_ref, own_ref, out_ref):
    lengths = len_ref[...].astype(F32)
    owner = own_ref[...]
    before = (
        lax.broadcasted_iota(jnp.int32, (S_TOT, S_TOT), 0)
        < lax.broadcasted_iota(jnp.int32, (S_TOT, S_TOT), 1)
    ).astype(F32).astype(BF16)
    lengths = jnp.broadcast_to(lengths, (8, S_TOT))
    starts = jnp.dot(lengths.astype(BF16), before, preferred_element_type=F32)
    owned = (lax.broadcasted_iota(jnp.int32, (N_CONTEXT, S_TOT), 0) == owner).astype(F32)
    earlier = jnp.dot(owned.astype(BF16), before, preferred_element_type=F32)
    slots = jnp.sum(owned * earlier, axis=0, keepdims=True).astype(jnp.int32)
    place = jnp.where(owner % NZ == ids[1], owner // NZ * SLOT_PAD + slots, -1)
    hit = (lax.broadcasted_iota(jnp.int32, (128, S_TOT), 0) == place).astype(F32).astype(BF16)
    high = jnp.floor(starts * (1.0 / 128.0))
    low = starts - high * 128.0
    row = lax.broadcasted_iota(jnp.int32, (8, S_TOT), 0)
    parts = jnp.where(row == 0, high, jnp.where(row == 1, low, lengths))
    placed = lax.dot_general(parts.astype(BF16), hit, DOT_LAST, preferred_element_type=F32)
    start = placed[0:1] * 128.0 + placed[1:2]
    end = start + placed[2:3]
    row_out = lax.broadcasted_iota(jnp.int32, (8, 128), 0)
    out_ref[...] = jnp.where(row_out == 0, start, end).astype(jnp.int32)


def pick_kernel(ids, q_ref, *out_refs):
    my_x, my_z, start = ids[0], ids[1], ids[2]
    row = lax.broadcasted_iota(jnp.int32, (ANS_X, SPAN), 0)
    lane = lax.broadcasted_iota(jnp.int32, (ANS_X, SPAN), 1)
    piece = PIECES - 1 - (my_x * NZ + my_z)
    for j in range(NX):
        other_x = lax.rem(my_x - j + NX, NX)
        pick = (piece * SPAN + lane == start + other_x * ANS_X + row).astype(F32).astype(BF16)
        out_refs[j][...] = jnp.dot(
            pick, q_ref[SPAN:TOK_DEV, :], preferred_element_type=F32
        ).astype(BF16)


def unit(queries, keys, values, state, index, visible):
    best, total, accum = state
    width = keys.shape[0]
    for rb in range(SET_ROWS // RB):
        rows = slice(rb * RB, (rb + 1) * RB)
        raw = lax.dot_general(queries(rows), keys, DOT_LAST, preferred_element_type=F32)
        parts = [raw[:, i * 128 : (i + 1) * 128] for i in range(width // 128)]
        if visible is not None:
            parts = [jnp.where(v, p, LOW) for v, p in zip(visible, parts)]
        top = functools.reduce(jnp.maximum, parts)
        old = best[index, rows, :]
        new = jnp.maximum(old, lanes(jnp.max(top, axis=1, keepdims=True)))
        alpha = jnp.exp2((old - new) * SCALE2)
        weights = [jnp.exp2((p - new) * SCALE2).astype(BF16) for p in parts]
        weights = jnp.concatenate(weights, axis=1)
        mixed = jnp.dot(weights, values, preferred_element_type=F32)
        best[index, rows, :] = new
        total[index, rows, :] = total[index, rows, :] * alpha + mixed[:, HEAD:]
        accum[index, rows, :] = accum[index, rows, :] * alpha + mixed[:, :HEAD]


def reset(state):
    best, total, accum = state
    best[...] = jnp.full_like(best, LOW)
    total[...] = jnp.zeros_like(total)
    accum[...] = jnp.zeros_like(accum)


def limits_to_masks(limits):
    row_w = lax.broadcasted_iota(jnp.int32, (RB, 128), 0) % SPAN
    offset = lax.broadcasted_iota(jnp.int32, (RB, 128), 1) - row_w
    return [offset <= limit for limit in limits]


def pack_logs(logs):
    flipped = logs.T[0:8, :]
    hi = flipped.astype(BF16)
    rest = flipped - hi.astype(F32)
    mid = rest.astype(BF16)
    lo = (rest - mid.astype(F32)).astype(BF16)
    return jnp.concatenate([hi, mid, lo], axis=1)


def read_logs(packed):
    packed = packed.astype(F32)
    return packed[:, :128] + packed[:, 128:256] + packed[:, 256:384]


def finish(state, index, write):
    best, total, accum = state
    lane = lax.broadcasted_iota(jnp.int32, (SPAN, 128), 1)
    logs = jnp.zeros((SPAN, 128), F32)
    for h in range(GROUP):
        rows = slice(h * SPAN, (h + 1) * SPAN)
        tot = jnp.maximum(total[index, rows, :], TINY)
        logs = jnp.where(lane == h, best[index, rows, :] * SCALE2 + jnp.log2(tot), logs)
        write(h, accum[index, rows, :] / tot)
    return pack_logs(logs)


def gather_keys(kv_ref, half, slots):
    blocks = [
        kv_ref[pl.ds(slot * TOK_DEV + pl.multiple_of(half * SPAN, SPAN), SPAN), :] for slot in slots
    ]
    ones = jnp.ones((len(blocks) * SPAN, HEAD), BF16)
    keys = jnp.concatenate([block[:, :HEAD] for block in blocks], axis=0)
    values = jnp.concatenate([block[:, HEAD:] for block in blocks], axis=0)
    return keys, jnp.concatenate([values, ones], axis=1)


def fold(state, into, index):
    best, total, accum = state
    for h in range(GROUP):
        rows = slice(h * SPAN, (h + 1) * SPAN)
        new = jnp.maximum(best[into, rows, :], best[index, rows, :])
        keep = jnp.exp2((best[into, rows, :] - new) * SCALE2)
        add = jnp.exp2((best[index, rows, :] - new) * SCALE2)
        total[into, rows, :] = total[into, rows, :] * keep + total[index, rows, :] * add
        accum[into, rows, :] = accum[into, rows, :] * keep + accum[index, rows, :] * add
        best[into, rows, :] = new
        best[index, rows, :] = jnp.full((SPAN, 128), LOW, F32)
        total[index, rows, :] = jnp.zeros((SPAN, 128), F32)
        accum[index, rows, :] = jnp.zeros((SPAN, HEAD), F32)


def spread(q_ref, qs):
    for half in range(2):
        for h in range(GROUP):
            qs[half, h * SPAN : (h + 1) * SPAN, :] = q_ref[
                half * SPAN : (half + 1) * SPAN, h * HEAD : (h + 1) * HEAD
            ]


def write_rows(state, msg_ref, base=0):
    for half in range(2):

        def write(h, value):
            msg_ref[half * SPAN : (half + 1) * SPAN, h * HEAD : (h + 1) * HEAD] = value.astype(BF16)

        msg_ref[TOK_DEV : TOK_DEV + 8, half * 384 : half * 384 + 384] = finish(
            state, base + half, write
        )


def peers_kernel(peers, *refs):
    count = len(peers)
    ids = refs[0]
    q_refs = refs[1 : 1 + count]
    kv_ref, tail_ref = refs[1 + count : 3 + count]
    msg_refs = refs[3 + count : 3 + 2 * count]
    qs = refs[3 + 2 * count]
    state = refs[4 + 2 * count :]
    my_x = ids[0]
    for i in range(count):
        spread(q_refs[i], qs.at[i])
    reset(state)

    def step(i, carry):
        j = peers[0] + i * (peers[-1] - peers[0])
        upper = (lax.rem(my_x - j + NX, NX) < my_x).astype(jnp.int32)
        keys, values = gather_keys(kv_ref, 0, range(NZ))
        unit(lambda rows: qs[i, 1, rows, :], keys, values, state, 2 * i + 1, None)
        keys, values = gather_keys(kv_ref, upper, range(NZ))
        unit(lambda rows: qs[i, upper, rows, :], keys, values, state, 2 * i, None)

        @pl.when(upper == 1)
        def _():
            fold(state, 2 * i + 1, 2 * i)

        return carry

    lax.fori_loop(0, count, step, 0)
    for i, j in enumerate(peers):
        write_rows(state, msg_refs[i], 2 * i)
        msg_refs[i][TOK_DEV + 8 : TOK_DEV + TAIL, :] = tail_ref[j, 8:TAIL, :]


def cited_kernel(*refs):
    ids, table = refs[0:2]
    a_refs = refs[2 : 2 + NX]
    kv_ref, tail_ref, qs, flat = refs[2 + NX : 6 + NX]
    state = refs[6 + NX :]
    my_x, start = ids[0], ids[2]
    other_x = [lax.rem(my_x - j + NX, NX) for j in range(NX)]
    for j in range(NX):
        for h in range(GROUP):
            at = pl.ds(pl.multiple_of(h * ANS + other_x[j] * ANS_X, ANS_X), ANS_X)
            qs[at, :] = a_refs[j][:, h * HEAD : (h + 1) * HEAD]
    col = lax.broadcasted_iota(jnp.int32, (SPAN, 128), 0)

    def bases(slot):
        context = my_x * NZ + slot
        return context * SPAN, (PIECES - 1 - context) * SPAN

    def tagged(half):
        keys, _ = gather_keys(kv_ref, half, range(NZ))
        tags = []
        for slot in range(NZ):
            place = bases(slot)[half] + col
            inside = jnp.logical_and(place >= table[0:1, :], place < table[1:2, :])
            tags.append(inside.astype(F32).astype(BF16))
        ones = jnp.ones((KEYS_HALF, HEAD), BF16)
        return keys, jnp.concatenate([jnp.concatenate(tags, axis=0), ones], axis=1)

    reset(state)
    keys, values = tagged(0)
    unit(lambda rows: qs[rows, :], keys, values, state, 0, None)
    keys, values = tagged(1)
    limits = [start - bases(slot)[1] for slot in range(NZ)]
    unit(lambda rows: qs[rows, :], keys, values, state, 1, limits_to_masks(limits))
    fold(state, 0, 1)

    def keep(h, value):
        flat[:, h * ANS : (h + 1) * ANS] = value.T.astype(BF16)

    logs = finish(state, 0, keep)
    for j in range(NX):
        tail_ref[j, 8:16, 0:384] = logs
        tail_ref[j, 16:TAIL, :] = flat[
            pl.ds(pl.multiple_of(other_x[j] * SLOT_PAD, SLOT_PAD), SLOT_PAD), :
        ]


def own_kernel(ids, q_ref, kv_ref, msg_ref, qs, *state):
    my_z = ids[1]
    per = NZ // 2
    spread(q_ref, qs)
    reset(state)
    keys, values = gather_keys(kv_ref, 0, range(NZ))
    unit(lambda rows: qs[1, rows, :], keys, values, state, 1, None)

    late = (my_z >= per).astype(jnp.int32)
    plain = 1 - late
    slots = [plain * per + i for i in range(per)]
    keys, values = gather_keys(kv_ref, plain, slots)
    unit(lambda rows: qs[plain, rows, :], keys, values, state, 2, None)

    slots = [late * per + i for i in range(per)]
    for half in range(2):
        limits = []
        for slot in slots:
            seen = slot < my_z if half == 0 else slot > my_z
            limits.append(jnp.where(slot == my_z, 0, jnp.where(seen, SPAN, -SPAN)))
        keys, values = gather_keys(kv_ref, half, slots)
        into = 0 if half == 0 else 3
        unit(lambda rows: qs[half, rows, :], keys, values, state, into, limits_to_masks(limits))
    fold(state, 1, 3)
    fold(state, plain, 2)
    write_rows(state, msg_ref)


def shares_of(logs):
    top = functools.reduce(jnp.maximum, logs)
    shares = [jnp.exp2(v - top) for v in logs]
    tot = functools.reduce(jnp.add, shares)
    return [v / tot for v in shares]


def combine_kernel(*refs):
    msgs, out_ref = refs[:NX], refs[NX]
    pad = jnp.zeros((SPAN - 8, SPAN), F32)
    for half in range(2):
        logs = slice(half * 384, half * 384 + 384)
        shares = shares_of([read_logs(m[TOK_DEV : TOK_DEV + 8, logs]) for m in msgs])
        flipped = [jnp.concatenate([v, pad], axis=0).T for v in shares]
        rows = slice(half * SPAN, (half + 1) * SPAN)
        for h in range(GROUP):
            cols = slice(h * HEAD, (h + 1) * HEAD)
            pieces = [
                m[rows, cols].astype(F32) * lanes(f[:, h : h + 1]) for m, f in zip(msgs, flipped)
            ]
            out_ref[rows, cols] = functools.reduce(jnp.add, pieces).astype(BF16)


def cite_kernel(ids, tail_ref, *refs):
    msgs, cite_ref = refs[: NX - 1], refs[NX - 1]
    tails = [tail_ref.at[0]] + [m.at[TOK_DEV : TOK_DEV + TAIL] for m in msgs]
    shares = shares_of([read_logs(t[8:16, 0:384]) for t in tails])
    value = jnp.zeros((SLOT_PAD, ANS), F32)
    for tail, share in zip(tails, shares):
        for h in range(GROUP):
            block = tail[16:TAIL, h * ANS : (h + 1) * ANS].astype(F32)
            value = value + block * share[h : h + 1, :]
    row = lax.broadcasted_iota(jnp.int32, (SLOT_PAD, ANS), 1)
    factor = (ids[2] + row + 1).astype(F32) * (SENT_DEV / (TOK_DEV * HEADS))
    value = value * factor
    rest = jnp.zeros((ANS - SLOT_PAD, ANS), F32)
    flipped = jnp.concatenate([value, rest], axis=0).T
    share = ANS // N_TENSOR
    for t in range(N_TENSOR):
        cite_ref[t] = flipped[t * share : (t + 1) * share, :]


VMEM_SPEC = pl.BlockSpec(memory_space=pltpu.VMEM)
SMEM_SPEC = pl.BlockSpec(memory_space=pltpu.SMEM)


def call(kernel, name, out_shape, scalars, arrays, scratch=(), flops=1e6, moved=1e6):
    many = isinstance(out_shape, list)
    return pl.pallas_call(
        kernel,
        out_shape=out_shape,
        in_specs=[SMEM_SPEC] * scalars + [VMEM_SPEC] * arrays,
        out_specs=[VMEM_SPEC] * len(out_shape) if many else VMEM_SPEC,
        scratch_shapes=list(scratch),
        compiler_params=pltpu.CompilerParams(vmem_limit_bytes=40 << 20),
        cost_estimate=pl.CostEstimate(
            flops=int(flops), bytes_accessed=int(moved), transcendentals=0
        ),
        name=name,
    )


def ring(count, step):
    return [(i, (i + step) % count) for i in range(count)]


def per_device(queries, key_states, value_states, sentence_lengths, sentence_owner, answer_start):
    my_x = lax.axis_index("x")
    my_z = lax.axis_index("z")
    ids = jnp.stack([my_x, my_z, answer_start[0]]).astype(jnp.int32)

    table = call(
        prep_kernel, "prep", jax.ShapeDtypeStruct((8, 128), jnp.int32), 1, 2, flops=3e8, moved=2e4
    )(ids, sentence_lengths.reshape(1, S_TOT), sentence_owner.reshape(1, S_TOT))

    pairs = lax.all_gather(
        jnp.concatenate([key_states, value_states], axis=1), "z", axis=0, tiled=True
    )
    q_all = [queries] + [lax.ppermute(queries, "x", ring(NX, j)) for j in (1, 2, 3)]
    part = jax.ShapeDtypeStruct((ANS_X, GROUP * HEAD), BF16)
    picked = call(pick_kernel, "pick", [part] * NX, 1, 1, flops=3e7)(ids, queries)
    asked = picked[0]
    for j in (1, 2, 3):
        asked = asked + lax.ppermute(picked[j], "x", ring(NX, -j))
    for shifts in ((8, 4, -4), (2, 1, -1)):
        got = [lax.ppermute(asked, "z", ring(NZ, s)) for s in shifts]
        asked = functools.reduce(jnp.add, got, asked)
    asked_all = [asked] + [lax.ppermute(asked, "x", ring(NX, j)) for j in (1, 2, 3)]

    width = GROUP * HEAD

    def state(sets):
        return [pltpu.VMEM((sets, SET_ROWS, 128), F32)] * 3

    tails = call(
        cited_kernel,
        "attend_cited",
        jax.ShapeDtypeStruct((NX, TAIL, width), BF16),
        1,
        NX + 2,
        [pltpu.VMEM((SET_ROWS, HEAD), BF16), pltpu.VMEM((128, GROUP * ANS), BF16)] + state(2),
        flops=2e9,
        moved=3e6,
    )(ids, table, *asked_all, pairs)
    got = [None] * NX
    for peers in ((2,), (1, 3)):
        msgs = call(
            functools.partial(peers_kernel, peers),
            "attend_peers",
            [jax.ShapeDtypeStruct((TOK_DEV + TAIL, width), BF16)] * len(peers),
            1,
            len(peers) + 2,
            [pltpu.VMEM((len(peers), 2, SET_ROWS, HEAD), BF16)] + state(2 * len(peers)),
            flops=2e9 * len(peers),
            moved=3e6,
        )(ids, *[q_all[j] for j in peers], pairs, tails)
        for j, msg in zip(peers, msgs):
            got[j] = lax.ppermute(msg, "x", ring(NX, -j))
    got[0] = call(
        own_kernel,
        "attend_own",
        jax.ShapeDtypeStruct((TOK_DEV + 16, width), BF16),
        1,
        2,
        [pltpu.VMEM((2, SET_ROWS, HEAD), BF16)] + state(4),
        flops=2e9,
        moved=3e6,
    )(ids, queries, pairs)
    got = lax.optimization_barrier(got)

    cited = call(
        cite_kernel,
        "cite",
        jax.ShapeDtypeStruct((N_TENSOR, ANS // N_TENSOR, ANS), F32),
        1,
        NX,
        flops=1e6,
        moved=1e6,
    )(ids, tails, *got[1:])
    attention = call(
        combine_kernel,
        "combine",
        jax.ShapeDtypeStruct((TOK_DEV, width), BF16),
        0,
        NX,
        flops=1e7,
        moved=3e6,
    )(*got)

    parts = jnp.sum(lax.all_to_all(cited, ("y", "core"), 0, 0), axis=0)
    citations = parts[:, :SENT_OWN].T
    return (attention, citations)


def solution(mesh):
    grid = Mesh(mesh.devices.reshape(NX, 2, NX, NZ), ("y", "core", "x", "z"))
    context, tensor = ("x", "z"), ("y", "core")
    return jax.shard_map(
        per_device,
        mesh=grid,
        in_specs=(
            P(context, tensor),
            P(context, tensor),
            P(context, tensor),
            P(),
            P(),
            P(),
        ),
        out_specs=(P(context, tensor), P(context, tensor)),
        check_vma=False,
    )
```
